32 devices in a mesh: groups: 2 (over x), rows: 16 (over z, y, core).
Axes of the slice: x: 2, y: 2, z: 4, core: 2. Of those that a mesh axis runs over, the one named last changes fastest.
Arguments:
- tokens: bfloat16 [128, 32, 1280], P(('groups', 'rows')), parts along dimension 0, may hold values from -6 to 6
- teacher_qkv: bfloat16 [128, 32, 480], P(('groups', 'rows')), parts along dimension 0, may hold values from -22 to 22
- s_qkv: bfloat16 [1280, 1920], P('rows')
- s_out: bfloat16 [640, 1280], P(None, 'rows'), may hold values from -0.25 to 0.25
- mlp_in: bfloat16 [1280, 2560], P('rows'), may hold values from -0.15625 to 0.15625
- mlp_out: bfloat16 [2560, 1280], P(None, 'rows'), may hold values from -0.125 to 0.125
- t_out: bfloat16 [160, 1280], P(None, 'rows'), may hold values from -0.5 to 0.5
Outputs:
- d_tokens: float32 [128, 32, 1280], P(('groups', 'rows')), parts along dimension 0
The draws below stay inside these ranges and needn't reach their ends.
There are 2 independent parts, one for each index of `groups`. The reference program is written for one: setup_inputs(seed, part) draws one part's arguments, and reference() takes and returns one part's arrays. A program takes and returns all parts, laid end to end along the dimension named above; an argument that names none is the same for every part. Nothing has to cross between parts.
All inputs are finite; a program needn't handle non-finite values.
Results may differ from the reference program's by a relative error of at most 0.019.
The reference program's roundings to bfloat16 on the way count: a program that leaves them out, or rounds other values in their place, can miss the bound.
Values may be sent and summed in bfloat16 or wider, within the bound.
No kernel may reach another device: no remote copies, remote signals or barrier semaphores. Data moves between devices by JAX's collectives and lax.ppermute only.
A program may use at most 128 MiB of HBM per device.

```python
import math
import jax
import jax.numpy as jnp
from jax import lax

D = 1280
HS = 8
HD = 80
TH = 2
HID = 2560
WIN = 8
TILE = 4
COLS = 32
IMG_ROWS = 64


def draw_tokens(key, part):
    first = jax.random.fold_in(key, 0)
    base = jax.random.truncated_normal(first, -6.0, 6.0, (IMG_ROWS, COLS, D), jnp.float32)
    return base.astype(jnp.bfloat16)


def draw_s_qkv(key, part):
    base = jax.random.truncated_normal(key, -4.0, 4.0, (D, 3 * HS * HD), jnp.float32) * D ** (-0.5)
    return base.astype(jnp.bfloat16)


def draw_teacher_qkv(key, part):
    first = jax.random.fold_in(key, 0)
    width = TH * HD
    total = IMG_ROWS * COLS
    base = jax.random.truncated_normal(first, -4.0, 4.0, (total, 3 * width), jnp.float32)
    column = jnp.arange(3 * width)[None, :]
    base = base * jnp.where(column < 2 * width, 1.6, 1.0)
    return base.reshape(IMG_ROWS, COLS, 3 * width).astype(jnp.bfloat16)


def level_of(stream_key, extent, cuts, low, high):
    def one(dim, blocks):
        steps = jax.random.uniform(jax.random.fold_in(jax.random.fold_in(stream_key, 6), dim), (blocks,), jnp.float32, low / len(cuts), high / len(cuts))
        return jnp.repeat(jnp.exp(steps), extent[dim] // blocks).reshape((-1,) + (1,) * (len(extent) - dim - 1))

    factor_of = one(*cuts[0])
    for cut in cuts[1:]:
        factor_of = factor_of * one(*cut)
    return factor_of


def scatter_about(key, dims, scale, reach, shards=(), kind=jnp.bfloat16):
    drawn = jax.random.normal(key, dims, jnp.float32) * scale
    if len(shards) > 0:
        drawn = level_of(key, dims, shards, -0.22, 0.18) * drawn
    return jnp.clip(drawn, min=-reach, max=reach).astype(kind)


def setup_inputs(seed: int = 0, part: int = 0) -> dict:
    splits = jax.random.split(jax.random.key(seed), 8)
    part_keys = jax.random.split(jax.random.fold_in(splits[7], part), 8)
    return {
        "tokens": draw_tokens(jax.random.fold_in(jax.random.fold_in(splits[7], part), 71), part),
        "teacher_qkv": draw_teacher_qkv(jax.random.fold_in(jax.random.fold_in(splits[7], part), 71), part),
        "s_qkv": draw_s_qkv(jax.random.fold_in(splits[7], 71), part),
        "s_out": scatter_about(splits[3], (HS * HD, D), (HS * HD) ** -0.5, 0.25, ((1, 16),)),
        "mlp_in": scatter_about(splits[4], (D, HID), D ** -0.5, 0.15625, ((0, 16),)),
        "mlp_out": scatter_about(splits[5], (HID, D), HID ** -0.5, 0.125, ((1, 16),)),
        "t_out": scatter_about(splits[6], (TH * HD, D), (TH * HD) ** -0.5, 0.5, ((1, 16),)),
    }


EPS = 1e-06

def norm_rows(values):
    centre = values - lax.optimization_barrier(jnp.mean(values, -1, keepdims=True))
    spread = lax.optimization_barrier(jnp.mean(centre * centre, -1, keepdims=True))
    return centre * lax.rsqrt(spread + EPS)

def norm_back(values, grads):
    centre = values - lax.optimization_barrier(jnp.mean(values, -1, keepdims=True))
    inverse = lax.rsqrt(lax.optimization_barrier(jnp.mean(centre * centre, -1, keepdims=True)) + EPS)
    normed = centre * inverse
    return inverse * (grads - lax.optimization_barrier(jnp.mean(grads, -1, keepdims=True)) - normed * lax.optimization_barrier(jnp.mean(grads * normed, -1, keepdims=True)))

def gelu_slope(values):
    return 0.5 * (1.0 + jax.scipy.special.erf(values / math.sqrt(2.0))) + values * jnp.exp(-0.5 * values * values) / math.sqrt(2.0 * math.pi)

def rounded_rim(values):
    narrow = lax.optimization_barrier(values.astype(jnp.bfloat16))
    return narrow.astype(jnp.float32)

def reference(tokens, teacher_qkv, s_qkv, s_out, mlp_in, mlp_out, t_out):
    rows_all, cols = (tokens.shape[0], tokens.shape[1])
    width = HS * HD
    half = WIN // 2
    scale = 1.0 / math.sqrt(HD)
    count = rows_all * cols
    flat_x = tokens.astype(jnp.float32).reshape(count, D)
    normed = norm_rows(flat_x).astype(jnp.bfloat16)
    packed = jnp.dot(normed, s_qkv, preferred_element_type=jnp.float32).astype(jnp.bfloat16)
    packed = packed.reshape(rows_all, cols, 3, HS, HD)
    query = packed[:, :, 0].astype(jnp.float32)
    key_pad = jnp.pad(packed[:, :, 1].astype(jnp.float32), ((half, half), (half, half), (0, 0), (0, 0)))
    val_pad = jnp.pad(packed[:, :, 2].astype(jnp.float32), ((half, half), (half, half), (0, 0), (0, 0)))
    row_id = jnp.arange(rows_all)[:, None]
    col_id = jnp.arange(cols)[None, :]
    offsets = [(row_off, col_off) for row_off in range(-half, half) for col_off in range(-half, half)]

    def shifted(padded, row_off, col_off):
        return padded[half + row_off:half + row_off + rows_all, half + col_off:half + col_off + cols]
    score_list = []
    for row_off, col_off in offsets:
        keys_here = shifted(key_pad, row_off, col_off)
        score = lax.optimization_barrier(jnp.sum(query * keys_here, -1)) * scale
        valid = (row_id + row_off >= 0) & (row_id + row_off < rows_all) & (col_id + col_off >= 0) & (col_id + col_off < cols)
        score_list.append(jnp.where(valid[:, :, None], score, -jnp.inf))
    scores = jnp.stack(score_list)
    peak = lax.optimization_barrier(jnp.max(scores, 0))
    expo = jnp.exp(scores - peak)
    probs = (expo / lax.optimization_barrier(jnp.sum(expo, 0))).astype(jnp.bfloat16)
    attn = jnp.zeros((rows_all, cols, HS, HD), jnp.float32)
    for index, (row_off, col_off) in enumerate(offsets):
        attn = attn + probs[index].astype(jnp.float32)[..., None] * shifted(val_pad, row_off, col_off)
    attn = attn.astype(jnp.bfloat16).reshape(count, width)
    resid = flat_x + jnp.dot(attn, s_out, preferred_element_type=jnp.float32)
    normed2 = norm_rows(resid).astype(jnp.bfloat16)
    pre = jnp.dot(normed2, mlp_in, preferred_element_type=jnp.float32)
    act = jax.nn.gelu(pre, approximate=False).astype(jnp.bfloat16)
    student = resid + jnp.dot(act, mlp_out, preferred_element_type=jnp.float32)
    teacher = teacher_qkv.reshape(count, 3, TH, HD).astype(jnp.float32)
    t_keys = teacher[:, 1]
    t_vals = teacher[:, 2]
    block = math.gcd(count, 1024)

    def teach_block(t_query):
        tscore = jnp.einsum('qhd,khd->hqk', t_query, t_keys) * scale
        tmax = lax.optimization_barrier(jnp.max(tscore, -1, keepdims=True))
        expo_t = jnp.exp(tscore - tmax)
        ttotal = lax.optimization_barrier(jnp.sum(expo_t, -1))
        tweight = expo_t.astype(jnp.bfloat16).astype(jnp.float32)
        summed = jnp.einsum('hqk,khd->qhd', tweight, t_vals)
        return summed / jnp.transpose(ttotal)[:, :, None]
    t_att = lax.map(teach_block, teacher[:, 0].reshape(count // block, block, TH, HD))
    t_att = t_att.reshape(count, TH * HD).astype(jnp.bfloat16)
    target = jnp.dot(t_att, t_out, preferred_element_type=jnp.float32)
    diff = student - target
    diff_b = diff.astype(jnp.bfloat16)
    dact = jnp.dot(diff_b, jnp.transpose(mlp_out), preferred_element_type=jnp.float32)
    dpre = (dact * gelu_slope(pre)).astype(jnp.bfloat16)
    dnorm2 = jnp.dot(dpre, jnp.transpose(mlp_in), preferred_element_type=jnp.float32)
    dresid = diff + norm_back(resid, dnorm2)
    dattn = jnp.dot(dresid.astype(jnp.bfloat16), jnp.transpose(s_out), preferred_element_type=jnp.float32)
    dattn = dattn.astype(jnp.bfloat16).astype(jnp.float32).reshape(rows_all, cols, HS, HD)
    dprob_list = []
    delta = jnp.zeros((rows_all, cols, HS), jnp.float32)
    for index, (row_off, col_off) in enumerate(offsets):
        dprob = lax.optimization_barrier(jnp.sum(dattn * shifted(val_pad, row_off, col_off), -1))
        dprob_list.append(dprob)
        delta = delta + probs[index].astype(jnp.float32) * dprob
    dquery = jnp.zeros((rows_all, cols, HS, HD), jnp.float32)
    key_own = jnp.zeros_like(key_pad)
    key_above = jnp.zeros_like(key_pad)
    key_below = jnp.zeros_like(key_pad)
    val_own = jnp.zeros_like(val_pad)
    val_above = jnp.zeros_like(val_pad)
    val_below = jnp.zeros_like(val_pad)
    row_tile = row_id // TILE
    for index, (row_off, col_off) in enumerate(offsets):
        prob_f = probs[index].astype(jnp.float32)
        dscore = (prob_f * (dprob_list[index] - delta)).astype(jnp.bfloat16).astype(jnp.float32)
        dquery = dquery + dscore[..., None] * shifted(key_pad, row_off, col_off)
        same_tile = ((row_id + row_off) // TILE == row_tile).astype(jnp.float32)[:, :, None, None]
        key_term = dscore[..., None] * query
        val_term = prob_f[..., None] * dattn
        row_lo = half + row_off
        col_lo = half + col_off
        key_own = key_own.at[row_lo:row_lo + rows_all, col_lo:col_lo + cols].add(key_term * same_tile)
        val_own = val_own.at[row_lo:row_lo + rows_all, col_lo:col_lo + cols].add(val_term * same_tile)
        if row_off > 0:
            key_above = key_above.at[row_lo:row_lo + rows_all, col_lo:col_lo + cols].add(key_term * (1.0 - same_tile))
            val_above = val_above.at[row_lo:row_lo + rows_all, col_lo:col_lo + cols].add(val_term * (1.0 - same_tile))
        elif row_off < 0:
            key_below = key_below.at[row_lo:row_lo + rows_all, col_lo:col_lo + cols].add(key_term * (1.0 - same_tile))
            val_below = val_below.at[row_lo:row_lo + rows_all, col_lo:col_lo + cols].add(val_term * (1.0 - same_tile))

    def inner(padded):
        return padded[half:half + rows_all, half:half + cols]
    dkey = inner(key_own) * scale + rounded_rim(inner(key_above) * scale) + rounded_rim(inner(key_below) * scale)
    dval = inner(val_own) + rounded_rim(inner(val_above)) + rounded_rim(inner(val_below))
    dqkv = jnp.stack([dquery * scale, dkey, dval], axis=2).astype(jnp.bfloat16).reshape(count, 3 * width)
    dnorm = jnp.dot(dqkv, jnp.transpose(s_qkv), preferred_element_type=jnp.float32)
    d_tokens = dresid + norm_back(flat_x, dnorm)
    return d_tokens.reshape(rows_all, cols, D)
```

```python
import functools
import math

import jax
import jax.numpy as jnp
from jax import lax
from jax.experimental import pallas as pl
from jax.experimental.pallas import tpu as pltpu
from jax.sharding import PartitionSpec as P


D = 1280
HS = 8
HD = 80
TH = 2
WIN = 8
LANES = 128


EPS = 1e-06


NN = (((1,), (0,)), ((), ()))
NT = (((1,), (1,)), ((), ()))
TN = (((0,), (0,)), ((), ()))


def mm(left, right, dims):
    return lax.dot_general(left, right, dims, preferred_element_type=jnp.float32)


def norm_parts(values):
    centre = values - jnp.mean(values, -1, keepdims=True)
    inverse = lax.rsqrt(jnp.mean(centre * centre, -1, keepdims=True) + EPS)
    return centre * inverse, inverse


def norm_back(values, grads):
    normed, inverse = norm_parts(values)
    return inverse * (
        grads
        - jnp.mean(grads, -1, keepdims=True)
        - normed * jnp.mean(grads * normed, -1, keepdims=True)
    )


def chip_at(place, chips):
    return 2 * place if place < chips // 2 else 2 * (chips - 1 - place) + 1


def ring_pairs(chips, step):
    pairs = []
    for place in range(chips):
        source, target = chip_at(place, chips), chip_at((place + step) % chips, chips)
        pairs += [(2 * source + core, 2 * target + core) for core in range(2)]
    return pairs


def ring(piece, chips, dim):
    forward, backward = ring_pairs(chips, 1), ring_pairs(chips, -1)
    reach = chips // 2
    cut = piece.shape[dim] // 2
    ups, downs = [piece], [piece]
    for _ in range(1, reach):
        ups.append(lax.ppermute(ups[-1], "rows", forward))
        downs.append(lax.ppermute(downs[-1], "rows", backward))
    last_up = lax.slice_in_dim(ups[-1], 0, cut, axis=dim)
    last_down = lax.slice_in_dim(downs[-1], cut, None, axis=dim)
    ups.append(lax.ppermute(last_up, "rows", forward))
    downs.append(lax.ppermute(last_down, "rows", backward))
    return ups[1:], downs[1:]


def slots_of(chips):
    reach = chips // 2
    steps = range(1, reach + 1)
    return [("u", k) for k in steps] + [("d", k) for k in steps]


def source_row(kind, k, chips, swap):
    me = lax.axis_index("rows")
    chip, core = lax.div(me, 2), lax.rem(me, 2)
    level = lax.div(chip, 2)
    place = jnp.where(lax.rem(chip, 2) == 0, level, chips - 1 - level)
    shift = {"o": 0, "u": chips - k, "d": k}[kind]
    at = lax.rem(place + shift, chips)
    source = jnp.where(at < chips // 2, 2 * at, 2 * (chips - 1 - at) + 1)
    return 2 * source + (1 - core if swap else core)


def column_copies(refs, dst, chips, height, width, lo, hi, swap, own):
    out = []
    slots = ([("o", 0)] if own else []) + slots_of(chips)
    for ref, (kind, k) in zip(refs, slots):
        first, last = 0, width
        if k == chips // 2:
            first, last = (0, width // 2) if kind == "u" else (width // 2, width)
        start, stop = max(lo, first), min(hi, last)
        if start >= stop:
            continue
        row = pl.multiple_of(source_row(kind, k, chips, swap) * height, 16)
        out.append(
            (
                ref.at[:, start - first : stop - first],
                dst.at[pl.ds(row, height), start - lo : stop - lo],
            )
        )
    return out


def row_copies(refs, dst, chips, total, keep, swap):
    out = []
    for ref, (kind, k) in zip(refs, [("o", 0)] + slots_of(chips)):
        first, last = 0, total
        if k == chips // 2:
            first, last = (0, total // 2) if kind == "u" else (total // 2, total)
        stop = min(keep, last)
        if first >= stop:
            continue
        row = pl.multiple_of(source_row(kind, k, chips, swap) * keep + first, 16)
        out.append((ref.at[0 : stop - first, :], dst.at[pl.ds(row, stop - first), :]))
    return out


def launch(copies, sems, base):
    started = []
    for i, (src, dst) in enumerate(copies):
        copy = pltpu.make_async_copy(src, dst, sems.at[base + i])
        copy.start()
        started.append(copy)
    return started


def finish(started):
    for copy in started:
        copy.wait()


ANY = pl.BlockSpec(memory_space=pl.ANY)
VM = pl.BlockSpec(memory_space=pltpu.VMEM)


def call(kernel, outs, scratch, vmem_mib, flops, moved, loose, tight):
    return pl.pallas_call(
        kernel,
        out_shape=outs,
        in_specs=[VM] * len(tight) + [ANY] * len(loose),
        out_specs=jax.tree.map(lambda _: VM, outs),
        scratch_shapes=scratch,
        cost_estimate=pl.CostEstimate(flops=flops, transcendentals=0, bytes_accessed=moved),
        compiler_params=pltpu.CompilerParams(vmem_limit_bytes=vmem_mib << 20),
    )(*tight, *loose)


def head_window(head):
    first, last = head * HD, (head + 1) * HD
    lo, hi = first // LANES * LANES, -(-last // LANES) * LANES
    return lo, hi


def head_mask(head, rows):
    lo, hi = head_window(head)
    lane = lax.broadcasted_iota(jnp.int32, (rows, hi - lo), 1) + lo
    return (lane >= head * HD) & (lane < (head + 1) * HD)


def qkv_kernel(chips, height, width, tok_ref, *refs):
    n = len(slots_of(chips)) + 1
    mine, other = refs[:n], refs[n : 2 * n]
    qkv_ref, w_ref, sems = refs[2 * n :]
    wide = w_ref.shape[1]
    copies = column_copies(mine, w_ref, chips, height, width, 0, wide, False, True)
    copies += column_copies(other, w_ref, chips, height, width, 0, wide, True, True)
    started = launch(copies, sems, 0)
    normed = norm_parts(tok_ref[...].astype(jnp.float32))[0].astype(jnp.bfloat16)
    finish(started)
    step = wide // 3
    for part in range(3):
        cols = slice(part * step, (part + 1) * step)
        qkv_ref[:, cols] = mm(normed, w_ref[:, cols], NN).astype(jnp.bfloat16)


def teacher_kernel(chips, rows, height, tq_ref, *refs):
    n = len(slots_of(chips)) + 1
    mine, other = refs[:n], refs[n : 2 * n]
    target_ref, all_ref, out_ref, sems = refs[2 * n :]
    copies = row_copies(mine, all_ref, chips, rows, rows, False)
    copies += row_copies(other, all_ref, chips, rows, rows, True)
    extra = row_copies(mine, out_ref, chips, rows, height, False)
    extra += row_copies(other, out_ref, chips, rows, height, True)
    started = launch(copies, sems, 0)
    later = launch(extra, sems, len(copies))
    finish(started)
    query = tq_ref[...]
    lane = lax.broadcasted_iota(jnp.int32, query.shape, 1)
    total = jnp.zeros(query.shape, jnp.float32)
    every = all_ref[...]
    for head in range(TH):
        here = (lane >= head * HD) & (lane < (head + 1) * HD)
        own = jnp.where(here, query, jnp.zeros_like(query))
        score = mm(own, every, NT) * (1.0 / math.sqrt(HD))
        expo = jnp.exp(score - jnp.max(score, -1, keepdims=True))
        summed = jnp.sum(expo, -1, keepdims=True)
        value = mm(expo.astype(jnp.bfloat16), every, NN) / summed
        first = (TH + head) * HD
        total = jnp.where((lane >= first) & (lane < first + HD), value, total)
    spread = pltpu.roll(total, TH * HD, axis=1).astype(jnp.bfloat16)
    finish(later)
    target_ref[...] = mm(spread, out_ref[...], NT)


def near_mask(count, cols, tile, last):
    half = WIN // 2
    shape = (count, 3 * count)
    query = lax.broadcasted_iota(jnp.int32, shape, 0)
    key = lax.broadcasted_iota(jnp.int32, shape, 1)
    row_off = lax.div(key, cols) - tile - lax.div(query, cols)
    col_off = lax.rem(key, cols) - lax.rem(query, cols)
    me = lax.axis_index("rows")
    row = me * tile + lax.div(key, cols) - tile
    valid = (row_off >= -half) & (row_off < half) & (col_off >= -half) & (col_off < half)
    return valid & (row >= 0) & (row < last)


def attention_kernel(chips, height, width, cols, tile, last, tok_ref, qkv_ref, lo_ref, hi_ref, *refs):
    n = len(slots_of(chips)) + 1
    mine, other = refs[:n], refs[n : 2 * n]
    probs_ref, resid_ref, normed_ref, w_ref, attn_ref, sems = refs[2 * n :]
    inner = HS * HD
    start = 3 * inner
    copies = column_copies(mine, w_ref, chips, height, width, start, width, False, True)
    copies += column_copies(other, w_ref, chips, height, width, start, width, True, True)
    started = launch(copies, sems, 0)
    count = qkv_ref.shape[0]
    valid = near_mask(count, cols, tile, last)
    attn_ref[...] = jnp.zeros_like(attn_ref)
    for head in range(HS):
        lo, hi = head_window(head)
        keep = head_mask(head, count)
        q = jnp.where(keep, qkv_ref[:, lo:hi], jnp.zeros((), jnp.bfloat16))
        k = jnp.concatenate(
            [lo_ref[:, lo:hi], qkv_ref[:, inner + lo : inner + hi], hi_ref[:, lo:hi]], axis=0
        )
        v = jnp.concatenate(
            [
                lo_ref[:, inner + lo : inner + hi],
                qkv_ref[:, 2 * inner + lo : 2 * inner + hi],
                hi_ref[:, inner + lo : inner + hi],
            ],
            axis=0,
        )
        score = jnp.where(valid, mm(q, k, NT) * (1.0 / math.sqrt(HD)), -jnp.inf)
        expo = jnp.exp(score - jnp.max(score, -1, keepdims=True))
        prob = (expo / jnp.sum(expo, -1, keepdims=True)).astype(jnp.bfloat16)
        probs_ref[head] = prob
        attn_ref[:, lo:hi] = jnp.where(keep, mm(prob, v, NN), attn_ref[:, lo:hi])
    finish(started)
    resid = tok_ref[...].astype(jnp.float32) + mm(attn_ref[...].astype(jnp.bfloat16), w_ref[...], NT)
    resid_ref[...] = resid
    normed_ref[...] = norm_parts(resid)[0].astype(jnp.bfloat16)


def main_kernel(
    chips,
    height,
    width,
    normed_ref,
    resid_ref,
    target_ref,
    qkv_ref,
    lo_ref,
    hi_ref,
    probs_ref,
    *refs,
):
    m = len(slots_of(chips))
    n = m + 1
    mine, other, refs = refs[:n], refs[n : 2 * n], refs[2 * n :]
    owned, refs = refs[:4], refs[4:]
    rings, refs = [refs[i * m : (i + 1) * m] for i in range(4)], refs[4 * m :]
    (dq_ref, own_ref, low_ref, high_ref, dresid_ref, b_ref, o_ref, slope_ref, acc_ref, dkv_ref, sems) = refs
    inner = HS * HD
    group = lax.axis_index("groups")
    copies = []
    for i, ref in enumerate(owned):
        row = pl.multiple_of(source_row("o", 0, chips, i >= 2) * height, 16)
        copies.append((ref.at[:, :], b_ref.at[i % 2, pl.ds(row, height), :]))
    for i, block in enumerate(rings):
        dst = b_ref.at[group if i % 2 == 0 else 1 - group]
        copies += column_copies(block, dst, chips, height, width, 0, width, i >= 2, False)
    started = launch(copies, sems, 0)
    extra = column_copies(mine, o_ref, chips, height, width, 3 * inner, width, False, True)
    extra += column_copies(other, o_ref, chips, height, width, 3 * inner, width, True, True)
    later = launch(extra, sems, len(copies))
    finish(started)

    count = normed_ref.shape[0]
    hidden = width
    step = 2 * 256
    normed = normed_ref[...]
    acc_ref[...] = resid_ref[...] - target_ref[...]

    def forward(j, carry):
        cols = pl.ds(pl.multiple_of(j * step, step), step)
        pre = mm(normed, b_ref[0, :, cols], NN)
        cdf = 0.5 * (1.0 + lax.erf(pre * (1.0 / math.sqrt(2.0))))
        act = (pre * cdf).astype(jnp.bfloat16)
        slope_ref[:, cols] = cdf + pre * jnp.exp(-0.5 * pre * pre) * (1.0 / math.sqrt(2.0 * math.pi))
        acc_ref[...] += mm(act, b_ref[1, :, cols], NT)
        return carry

    lax.fori_loop(0, hidden // step, forward, 0)
    diff = acc_ref[...]
    dresid_ref[...] = diff
    diff_b = diff.astype(jnp.bfloat16)
    acc_ref[...] = jnp.zeros_like(acc_ref)

    def backward(j, carry):
        cols = pl.ds(pl.multiple_of(j * step, step), step)
        dact = mm(diff_b, b_ref[1, :, cols], NN)
        dpre = (dact * slope_ref[:, cols]).astype(jnp.bfloat16)
        acc_ref[...] += mm(dpre, b_ref[0, :, cols], NT)
        return carry

    lax.fori_loop(0, hidden // step, backward, 0)
    dresid = dresid_ref[...] + norm_back(resid_ref[...], acc_ref[...])
    dresid_ref[...] = dresid
    finish(later)
    dattn = mm(dresid.astype(jnp.bfloat16), o_ref[...], NN).astype(jnp.bfloat16)
    dkv_ref[...] = jnp.zeros_like(dkv_ref)
    dq_ref[...] = jnp.zeros_like(dq_ref)
    scale = 1.0 / math.sqrt(HD)
    zero = jnp.zeros((), jnp.bfloat16)
    for head in range(HS):
        lo, hi = head_window(head)
        keep = head_mask(head, count)
        q = jnp.where(keep, qkv_ref[:, lo:hi], zero)
        da = jnp.where(keep, dattn[:, lo:hi], zero)
        k = jnp.concatenate(
            [lo_ref[:, lo:hi], qkv_ref[:, inner + lo : inner + hi], hi_ref[:, lo:hi]], axis=0
        )
        v = jnp.concatenate(
            [
                lo_ref[:, inner + lo : inner + hi],
                qkv_ref[:, 2 * inner + lo : 2 * inner + hi],
                hi_ref[:, inner + lo : inner + hi],
            ],
            axis=0,
        )
        prob = probs_ref[head]
        prob_f = prob.astype(jnp.float32)
        dprob = mm(da, v, NT)
        delta = jnp.sum(prob_f * dprob, -1, keepdims=True)
        dscore = (prob_f * (dprob - delta)).astype(jnp.bfloat16)
        dq = (mm(dscore, k, NN) * scale).astype(jnp.bfloat16)
        dq_ref[:, lo:hi] = jnp.where(keep, dq, dq_ref[:, lo:hi])
        dkv_ref[:, lo:hi] += mm(dscore, q, TN) * scale
        dkv_ref[:, inner + lo : inner + hi] += mm(prob, da, TN)
    low_ref[...] = dkv_ref[0:count, :].astype(jnp.bfloat16)
    own_ref[...] = dkv_ref[count : 2 * count, :]
    high_ref[...] = dkv_ref[2 * count :, :].astype(jnp.bfloat16)


def final_kernel(
    chips, height, width, tok_ref, dresid_ref, dq_ref, own_ref, above_ref, below_ref, *refs
):
    n = len(slots_of(chips)) + 1
    mine, other = refs[:n], refs[n : 2 * n]
    out_ref, w_ref, sems = refs[2 * n :]
    wide = w_ref.shape[1]
    copies = column_copies(mine, w_ref, chips, height, width, 0, wide, False, True)
    copies += column_copies(other, w_ref, chips, height, width, 0, wide, True, True)
    started = launch(copies, sems, 0)
    dkv = own_ref[...] + above_ref[...].astype(jnp.float32) + below_ref[...].astype(jnp.float32)
    dkv = dkv.astype(jnp.bfloat16)
    finish(started)
    inner = HS * HD
    dnorm = mm(dq_ref[...], w_ref[:, :inner], NT) + mm(dkv, w_ref[:, inner:], NT)
    out_ref[...] = dresid_ref[...] + norm_back(tok_ref[...].astype(jnp.float32), dnorm)


def body(mesh, tokens, teacher_qkv, s_qkv, s_out, mlp_in, mlp_out, t_out):
    return fast_body(mesh, tokens, teacher_qkv, s_qkv, s_out, mlp_in, mlp_out, t_out)


def fast_body(mesh, tokens, teacher_qkv, s_qkv, s_out, mlp_in, mlp_out, t_out):
    tile, cols, dim = tokens.shape
    devices = mesh.shape["rows"]
    chips = devices // 2
    count = tile * cols
    inner = HS * HD
    height = s_qkv.shape[0]
    width = mlp_in.shape[1]
    hidden = width
    bf, f32 = jnp.bfloat16, jnp.float32
    group = lax.axis_index("groups")
    partner = [(i, i ^ 1) for i in range(devices)]
    across = [(0, 1), (1, 0)]

    tok = tokens.reshape(count, dim)
    teacher = teacher_qkv.reshape(count, 3 * TH * HD)
    down = mlp_out.T
    b0 = jnp.where(group == 0, mlp_in, down)
    a0 = jnp.concatenate([s_qkv, s_out.T], axis=1)
    lanes = -(-3 * TH * HD // LANES) * LANES
    t_rows = jnp.pad(t_out.T, ((0, count - height), (0, lanes - 3 * TH * HD)))
    t0 = jnp.concatenate([teacher[:, TH * HD :], t_rows], axis=1)
    tq = jnp.pad(teacher[:, : TH * HD], ((0, 0), (0, lanes - TH * HD)))

    bu, bd = ring(b0, chips, 1)
    au, ad = ring(a0, chips, 1)
    tu, td = ring(t0, chips, 0)
    xu = [lax.ppermute(x, "groups", across) for x in bu]
    xd = [lax.ppermute(x, "groups", across) for x in bd]

    def swap(values):
        return [lax.ppermute(x, "rows", partner) for x in values]

    t_mine = [t0] + tu + td
    a_mine = [a0] + au + ad
    t_other = swap(t_mine)
    a_other = swap(a_mine)
    owned = [mlp_in, down]
    owned_other = swap(owned)
    b_other = swap(bu + bd)
    x_other = swap(xu + xd)
    slots = len(slots_of(chips)) + 1

    target = call(
        functools.partial(teacher_kernel, chips, count, height),
        jax.ShapeDtypeStruct((count, dim), f32),
        [
            pltpu.VMEM((devices * count, lanes), bf),
            pltpu.VMEM((dim, lanes), bf),
            pltpu.SemaphoreType.DMA((4 * slots,)),
        ],
        24,
        4 * TH * count * devices * count * lanes,
        2 * devices * count * lanes,
        t_mine + t_other,
        [tq],
    )
    qkv = call(
        functools.partial(qkv_kernel, chips, height, width),
        jax.ShapeDtypeStruct((count, 3 * inner), bf),
        [pltpu.VMEM((dim, 3 * inner), bf), pltpu.SemaphoreType.DMA((2 * slots,))],
        16,
        2 * count * dim * 3 * inner,
        2 * dim * 3 * inner,
        a_mine + a_other,
        [tok],
    )
    key_val = qkv[:, inner:]
    upward = [(i, i + 1) for i in range(devices - 1)]
    downward = [(i + 1, i) for i in range(devices - 1)]
    low = lax.ppermute(key_val, "rows", upward)
    high = lax.ppermute(key_val, "rows", downward)
    probs, resid, normed2 = call(
        functools.partial(
            attention_kernel, chips, height, width, cols, tile, devices * tile
        ),
        (
            jax.ShapeDtypeStruct((HS, count, 3 * count), bf),
            jax.ShapeDtypeStruct((count, dim), f32),
            jax.ShapeDtypeStruct((count, dim), bf),
        ),
        [
            pltpu.VMEM((dim, inner), bf),
            pltpu.VMEM((count, inner), f32),
            pltpu.SemaphoreType.DMA((2 * slots,)),
        ],
        16,
        2 * count * dim * inner + 4 * HS * count * 3 * count * 2 * LANES,
        2 * dim * inner + 2 * HS * count * 3 * count,
        a_mine + a_other,
        [tok, qkv, low, high],
    )
    blocks = bu + bd + xu + xd + b_other + x_other
    dq, own, to_above, to_below, dresid = call(
        functools.partial(main_kernel, chips, height, width),
        (
            jax.ShapeDtypeStruct((count, inner), bf),
            jax.ShapeDtypeStruct((count, 2 * inner), f32),
            jax.ShapeDtypeStruct((count, 2 * inner), bf),
            jax.ShapeDtypeStruct((count, 2 * inner), bf),
            jax.ShapeDtypeStruct((count, dim), f32),
        ),
        [
            pltpu.VMEM((2, dim, hidden), bf),
            pltpu.VMEM((dim, inner), bf),
            pltpu.VMEM((count, hidden), f32),
            pltpu.VMEM((count, dim), f32),
            pltpu.VMEM((3 * count, 2 * inner), f32),
            pltpu.SemaphoreType.DMA((8 * slots,)),
        ],
        36,
        8 * count * dim * hidden,
        4 * dim * hidden,
        a_mine + a_other + owned + owned_other + blocks,
        [normed2, resid, target, qkv, low, high, probs],
    )
    from_above = lax.ppermute(to_below, "rows", upward)
    from_below = lax.ppermute(to_above, "rows", downward)
    d_tokens = call(
        functools.partial(final_kernel, chips, height, width),
        jax.ShapeDtypeStruct((count, dim), f32),
        [pltpu.VMEM((dim, 3 * inner), bf), pltpu.SemaphoreType.DMA((2 * slots,))],
        20,
        2 * count * dim * 3 * inner,
        2 * dim * 3 * inner,
        a_mine + a_other,
        [tok, dresid, dq, own, from_above, from_below],
    )
    return d_tokens.reshape(tile, cols, dim)


def extended_2(block, sides, width):
    for axis, dim in sides:
        count = lax.axis_size(axis)
        forward = [(i, i + 1) for i in range(count - 1)]
        backward = [(target, source) for source, target in forward]
        low = lax.ppermute(
            lax.slice_in_dim(block, block.shape[dim] - width, None, axis=dim), axis, forward
        )
        high = lax.ppermute(lax.slice_in_dim(block, 0, width, axis=dim), axis, backward)
        block = jnp.concatenate([low, block, high], axis=dim)
    return block


def from_behind(value, axis, by):
    length = lax.axis_size(axis)
    pairs = [(i, i + by) for i in range(length) if 0 <= i + by < length]
    return lax.ppermute(value, axis, pairs)


def gelu_slope(values):
    return 0.5 * (1.0 + jax.scipy.special.erf(values / math.sqrt(2.0))) + values * jnp.exp(
        -0.5 * values * values
    ) / math.sqrt(2.0 * math.pi)


def plain_body(tokens, teacher_qkv, s_qkv, s_out, mlp_in, mlp_out, t_out):
    tile, cols = (tokens.shape[0], tokens.shape[1])
    width = HS * HD
    half = WIN // 2
    scale = 1.0 / math.sqrt(HD)
    count = tile * cols
    w_qkv, w_out, w_in, w_down, w_teach = (
        lax.all_gather(s_qkv, "rows", axis=0, tiled=True),
        lax.all_gather(s_out, "rows", axis=1, tiled=True),
        lax.all_gather(mlp_in, "rows", axis=0, tiled=True),
        lax.all_gather(mlp_out, "rows", axis=1, tiled=True),
        lax.all_gather(t_out, "rows", axis=1, tiled=True),
    )
    flat_x = tokens.astype(jnp.float32).reshape(count, D)
    normed = norm_parts(flat_x)[0].astype(jnp.bfloat16)
    packed = jnp.dot(normed, w_qkv, preferred_element_type=jnp.float32).astype(jnp.bfloat16)
    packed = packed.reshape(tile, cols, 3 * width)
    query = packed[:, :, :width].reshape(count, HS, HD)
    key_val = packed[:, :, width:]
    extended = extended_2(key_val, (("rows", 0),), half)
    extended = jnp.pad(extended, ((0, 0), (half, half), (0, 0)))
    key_rows = tile + 2 * half
    key_cols = cols + 2 * half
    key_count = key_rows * key_cols
    both = extended.reshape(key_count, 2, HS, HD)
    keys_all = both[:, 0]
    vals_all = both[:, 1]
    query_row = (jnp.arange(count) // cols)[:, None]
    query_col = (jnp.arange(count) % cols)[:, None]
    key_row = (jnp.arange(key_count) // key_cols)[None, :]
    key_col = (jnp.arange(key_count) % key_cols)[None, :]
    row_off = key_row - half - query_row
    col_off = key_col - half - query_col
    global_row = lax.axis_index("rows") * tile + query_row + row_off
    valid = (row_off >= -half) & (row_off < half) & (col_off >= -half) & (col_off < half)
    valid = valid & (global_row >= 0) & (global_row < lax.axis_size("rows") * tile)
    valid = valid & (query_col + col_off >= 0) & (query_col + col_off < cols)
    scores = jnp.einsum("qhd,khd->hqk", query, keys_all, preferred_element_type=jnp.float32) * scale
    scores = jnp.where(valid[None], scores, -jnp.inf)
    peak = jnp.max(scores, -1, keepdims=True)
    expo = jnp.exp(scores - peak)
    probs = (expo / jnp.sum(expo, -1, keepdims=True)).astype(jnp.bfloat16)
    attn = jnp.einsum("hqk,khd->qhd", probs, vals_all, preferred_element_type=jnp.float32)
    attn = attn.astype(jnp.bfloat16).reshape(count, width)
    resid = flat_x + jnp.dot(attn, w_out, preferred_element_type=jnp.float32)
    teacher = teacher_qkv.reshape(count, 3 * TH * HD)
    t_query = teacher[:, : TH * HD].reshape(count, TH, HD)
    t_pairs = teacher[:, TH * HD :]
    piece = lax.all_gather(t_pairs, "rows", axis=0, tiled=True)
    run_max = jnp.full((TH, count), -1e30, jnp.float32)
    piece_kv = piece.reshape(piece.shape[0], 2, TH, HD)
    tscore = (
        jnp.einsum("qhd,khd->hqk", t_query, piece_kv[:, 0], preferred_element_type=jnp.float32)
        * scale
    )
    new_max = jnp.maximum(run_max, jnp.max(tscore, -1))
    expo_t = jnp.exp(tscore - new_max[..., None])
    new_total = jnp.sum(expo_t, -1)
    added = jnp.einsum(
        "hqk,khd->qhd",
        expo_t.astype(jnp.bfloat16),
        piece_kv[:, 1],
        preferred_element_type=jnp.float32,
    )
    t_att = (
        (added / jnp.transpose(new_total)[:, :, None]).astype(jnp.bfloat16).reshape(count, TH * HD)
    )
    target = jnp.dot(t_att, w_teach, preferred_element_type=jnp.float32)
    normed2 = norm_parts(resid)[0].astype(jnp.bfloat16)
    pre = jnp.dot(normed2, w_in, preferred_element_type=jnp.float32)
    act = jax.nn.gelu(pre, approximate=False).astype(jnp.bfloat16)
    student = resid + jnp.dot(act, w_down, preferred_element_type=jnp.float32)
    diff = student - target
    diff_b = diff.astype(jnp.bfloat16)
    dact = jnp.einsum("nd,hd->nh", diff_b, w_down, preferred_element_type=jnp.float32)
    dpre = (dact * gelu_slope(pre)).astype(jnp.bfloat16)
    dnorm2 = jnp.einsum("nh,dh->nd", dpre, w_in, preferred_element_type=jnp.float32)
    dresid = diff + norm_back(resid, dnorm2)
    dattn = jnp.einsum(
        "nd,ad->na", dresid.astype(jnp.bfloat16), w_out, preferred_element_type=jnp.float32
    )
    dattn = dattn.astype(jnp.bfloat16).reshape(count, HS, HD)
    dprob = jnp.einsum("qhd,khd->hqk", dattn, vals_all, preferred_element_type=jnp.float32)
    delta = jnp.sum(probs.astype(jnp.float32) * dprob, -1, keepdims=True)
    dscore = (probs.astype(jnp.float32) * (dprob - delta)).astype(jnp.bfloat16)
    dquery = (
        jnp.einsum("hqk,khd->qhd", dscore, keys_all, preferred_element_type=jnp.float32) * scale
    )
    dkey = jnp.einsum("hqk,qhd->khd", dscore, query, preferred_element_type=jnp.float32) * scale
    dval = jnp.einsum("hqk,qhd->khd", probs, dattn, preferred_element_type=jnp.float32)
    grad_kv = jnp.concatenate(
        [dkey.reshape(key_count, width), dval.reshape(key_count, width)], axis=-1
    )
    grad_kv = grad_kv.reshape(key_rows, key_cols, 2 * width)[:, half : half + cols]
    top_rim = grad_kv[:half].astype(jnp.bfloat16)
    bottom_rim = grad_kv[half + tile :].astype(jnp.bfloat16)
    own_rows = grad_kv[half : half + tile]
    from_above = from_behind(bottom_rim, "rows", 1)
    from_below = from_behind(top_rim, "rows", -1)
    own_rows = own_rows.at[:half].add(from_above.astype(jnp.float32))
    own_rows = own_rows.at[tile - half :].add(from_below.astype(jnp.float32))
    dqkv = jnp.concatenate(
        [dquery.reshape(count, width), own_rows.reshape(count, 2 * width)], axis=-1
    ).astype(jnp.bfloat16)
    dnorm = jnp.einsum("ne,de->nd", dqkv, w_qkv, preferred_element_type=jnp.float32)
    d_tokens = dresid + norm_back(flat_x, dnorm)
    return d_tokens.reshape(tile, cols, D)


def fits(mesh, shapes):
    devices = mesh.shape["rows"]
    return (
        mesh.shape["groups"] == 2
        and devices % 4 == 0
        and D % (16 * devices) == 0
        and shapes == WIN // 2
    )


def solution(mesh):
    placed = (
        P(("groups", "rows"), None, None),
        P(("groups", "rows"), None, None),
        P("rows", None),
        P(None, "rows"),
        P("rows", None),
        P(None, "rows"),
        P(None, "rows"),
    )

    def chosen(tokens, *rest):
        tile = tokens.shape[0] // (mesh.shape["groups"] * mesh.shape["rows"])
        fast = fits(mesh, tile)
        step = jax.shard_map(
            functools.partial(body, mesh) if fast else plain_body,
            mesh=mesh,
            in_specs=placed,
            out_specs=P(("groups", "rows"), None, None),
            check_vma=False,
        )
        return step(tokens, *rest)

    return chosen
```

```python
import functools
import math

import jax
import jax.numpy as jnp
from jax import lax
from jax.experimental import pallas as pl
from jax.experimental.pallas import tpu as pltpu
from jax.sharding import PartitionSpec as P


D = 1280
HS = 8
HD = 80
TH = 2
WIN = 8
LANES = 128


EPS = 1e-06


NN = (((1,), (0,)), ((), ()))
NT = (((1,), (1,)), ((), ()))
TN = (((0,), (0,)), ((), ()))


def mm(left, right, dims):
    return lax.dot_general(left, right, dims, preferred_element_type=jnp.float32)


def norm_parts(values):
    centre = values - jnp.mean(values, -1, keepdims=True)
    inverse = lax.rsqrt(jnp.mean(centre * centre, -1, keepdims=True) + EPS)
    return centre * inverse, inverse


def norm_back(values, grads):
    normed, inverse = norm_parts(values)
    return inverse * (
        grads
        - jnp.mean(grads, -1, keepdims=True)
        - normed * jnp.mean(grads * normed, -1, keepdims=True)
    )


def chip_at(place, chips):
    return 2 * place if place < chips // 2 else 2 * (chips - 1 - place) + 1


def ring_pairs(chips, step):
    pairs = []
    for place in range(chips):
        source, target = chip_at(place, chips), chip_at((place + step) % chips, chips)
        pairs += [(2 * source + core, 2 * target + core) for core in range(2)]
    return pairs


def ring(piece, chips, dim):
    forward, backward = ring_pairs(chips, 1), ring_pairs(chips, -1)
    reach = chips // 2
    cut = piece.shape[dim] // 2
    ups, downs = [piece], [piece]
    for _ in range(1, reach):
        ups.append(lax.ppermute(ups[-1], "rows", forward))
        downs.append(lax.ppermute(downs[-1], "rows", backward))
    last_up = lax.slice_in_dim(ups[-1], 0, cut, axis=dim)
    last_down = lax.slice_in_dim(downs[-1], cut, None, axis=dim)
    ups.append(lax.ppermute(last_up, "rows", forward))
    downs.append(lax.ppermute(last_down, "rows", backward))
    return ups[1:], downs[1:]


def mine_count(chips):
    return 1 + chips // 2 * 2


def other_count(chips):
    return 1 + chips // 2


def source_row(kind, k, chips, swap):
    me = lax.axis_index("rows")
    chip, core = lax.div(me, 2), lax.rem(me, 2)
    level = lax.div(chip, 2)
    place = jnp.where(lax.rem(chip, 2) == 0, level, chips - 1 - level)
    shift = {"o": 0, "u": chips - k, "d": k, "f": k}[kind]
    at = lax.rem(place + shift, chips)
    source = jnp.where(at < chips // 2, 2 * at, 2 * (chips - 1 - at) + 1)
    return 2 * source + (1 - core if swap else core)


def pieces(refs, chips, merged, own):
    reach = chips // 2
    out = []
    refs = list(refs)
    if own:
        out.append(("o", 0, refs.pop(0)))
    if not merged:
        slots = [("u", k) for k in range(1, reach + 1)] + [("d", k) for k in range(1, reach + 1)]
        return out + [(kind, k, ref) for (kind, k), ref in zip(slots, refs)]
    for k, ref in zip(range(1, reach), refs):
        rows = ref.shape[0] // 2
        out += [("u", k, ref.at[0:rows]), ("d", k, ref.at[rows : 2 * rows])]
    return out + [("f", reach, refs[-1])]


def column_copies(refs, dst, chips, height, width, lo, hi, merged, own):
    out = []
    for kind, k, ref in pieces(refs, chips, merged, own):
        first, last = 0, width
        if k == chips // 2 and kind != "f":
            first, last = (0, width // 2) if kind == "u" else (width // 2, width)
        start, stop = max(lo, first), min(hi, last)
        if start >= stop:
            continue
        row = pl.multiple_of(source_row(kind, k, chips, merged) * height, 16)
        out.append(
            (
                ref.at[:, start - first : stop - first],
                dst.at[pl.ds(row, height), start - lo : stop - lo],
            )
        )
    return out


def row_copies(refs, dst, chips, total, keep, merged):
    out = []
    for kind, k, ref in pieces(refs, chips, merged, True):
        first, last = 0, total
        if k == chips // 2 and kind != "f":
            first, last = (0, total // 2) if kind == "u" else (total // 2, total)
        stop = min(keep, last)
        if first >= stop:
            continue
        row = pl.multiple_of(source_row(kind, k, chips, merged) * keep + first, 16)
        out.append((ref.at[0 : stop - first, :], dst.at[pl.ds(row, stop - first), :]))
    return out


def launch(copies, sems, base):
    started = []
    for i, (src, dst) in enumerate(copies):
        copy = pltpu.make_async_copy(src, dst, sems.at[base + i])
        copy.start()
        started.append(copy)
    return started


def finish(started):
    for copy in started:
        copy.wait()


ANY = pl.BlockSpec(memory_space=pl.ANY)
VM = pl.BlockSpec(memory_space=pltpu.VMEM)


def call(kernel, outs, scratch, vmem_mib, flops, moved, loose, tight):
    return pl.pallas_call(
        kernel,
        out_shape=outs,
        in_specs=[VM] * len(tight) + [ANY] * len(loose),
        out_specs=jax.tree.map(lambda _: VM, outs),
        scratch_shapes=scratch,
        cost_estimate=pl.CostEstimate(flops=flops, transcendentals=0, bytes_accessed=moved),
        compiler_params=pltpu.CompilerParams(vmem_limit_bytes=vmem_mib << 20),
    )(*tight, *loose)


def head_window(head):
    first, last = head * HD, (head + 1) * HD
    lo, hi = first // LANES * LANES, -(-last // LANES) * LANES
    return lo, hi


def head_mask(head, rows):
    lo, hi = head_window(head)
    lane = lax.broadcasted_iota(jnp.int32, (rows, hi - lo), 1) + lo
    return (lane >= head * HD) & (lane < (head + 1) * HD)


def split(refs, chips):
    n, m = mine_count(chips), other_count(chips)
    return refs[:n], refs[n : n + m], refs[n + m :]


def qkv_kernel(chips, height, width, tok_ref, lo_ref, hi_ref, *refs):
    mine, other, refs = split(refs, chips)
    q_ref, kv_ref, w_ref, sems = refs
    wide = w_ref.shape[1]
    copies = column_copies(mine, w_ref, chips, height, width, 0, wide, False, True)
    copies += column_copies(other, w_ref, chips, height, width, 0, wide, True, True)
    started = launch(copies, sems, 0)
    normed = [
        norm_parts(ref[...].astype(jnp.float32))[0].astype(jnp.bfloat16)
        for ref in (lo_ref, tok_ref, hi_ref)
    ]
    finish(started)
    inner = wide // 3
    q_ref[...] = mm(normed[1], w_ref[:, :inner], NN).astype(jnp.bfloat16)
    rows = jnp.concatenate(normed, axis=0)
    for part in range(2):
        cols = slice(part * inner, (part + 1) * inner)
        weights = w_ref[:, (part + 1) * inner : (part + 2) * inner]
        kv_ref[:, cols] = mm(rows, weights, NN).astype(jnp.bfloat16)


def teacher_kernel(chips, rows, height, tq_ref, *refs):
    mine, other, refs = split(refs, chips)
    target_ref, all_ref, out_ref, sems = refs
    copies = row_copies(mine, all_ref, chips, rows, rows, False)
    copies += row_copies(other, all_ref, chips, rows, rows, True)
    extra = row_copies(mine, out_ref, chips, rows, height, False)
    extra += row_copies(other, out_ref, chips, rows, height, True)
    started = launch(copies, sems, 0)
    later = launch(extra, sems, len(copies))
    finish(started)
    query = tq_ref[...]
    lane = lax.broadcasted_iota(jnp.int32, query.shape, 1)
    total = jnp.zeros(query.shape, jnp.float32)
    every = all_ref[...]
    for head in range(TH):
        here = (lane >= head * HD) & (lane < (head + 1) * HD)
        own = jnp.where(here, query, jnp.zeros_like(query))
        score = mm(own, every, NT) * (1.0 / math.sqrt(HD))
        expo = jnp.exp(score - jnp.max(score, -1, keepdims=True))
        summed = jnp.sum(expo, -1, keepdims=True)
        value = mm(expo.astype(jnp.bfloat16), every, NN) / summed
        first = (TH + head) * HD
        total = jnp.where((lane >= first) & (lane < first + HD), value, total)
    spread = pltpu.roll(total, TH * HD, axis=1).astype(jnp.bfloat16)
    finish(later)
    target_ref[...] = mm(spread, out_ref[...], NT)


def near_mask(count, cols, tile, last):
    half = WIN // 2
    shape = (count, 3 * count)
    query = lax.broadcasted_iota(jnp.int32, shape, 0)
    key = lax.broadcasted_iota(jnp.int32, shape, 1)
    row_off = lax.div(key, cols) - tile - lax.div(query, cols)
    col_off = lax.rem(key, cols) - lax.rem(query, cols)
    me = lax.axis_index("rows")
    row = me * tile + lax.div(key, cols) - tile
    valid = (row_off >= -half) & (row_off < half) & (col_off >= -half) & (col_off < half)
    return valid & (row >= 0) & (row < last)


def attention_kernel(chips, height, width, cols, tile, last, tok_ref, q_ref, kv_ref, *refs):
    mine, other, refs = split(refs, chips)
    probs_ref, resid_ref, normed_ref, w_ref, attn_ref, sems = refs
    inner = HS * HD
    start = 3 * inner
    copies = column_copies(mine, w_ref, chips, height, width, start, width, False, True)
    copies += column_copies(other, w_ref, chips, height, width, start, width, True, True)
    started = launch(copies, sems, 0)
    count = q_ref.shape[0]
    valid = near_mask(count, cols, tile, last)
    attn_ref[...] = jnp.zeros_like(attn_ref)
    for head in range(HS):
        lo, hi = head_window(head)
        keep = head_mask(head, count)
        q = jnp.where(keep, q_ref[:, lo:hi], jnp.zeros((), jnp.bfloat16))
        k = kv_ref[:, lo:hi]
        v = kv_ref[:, inner + lo : inner + hi]
        score = jnp.where(valid, mm(q, k, NT) * (1.0 / math.sqrt(HD)), -jnp.inf)
        expo = jnp.exp(score - jnp.max(score, -1, keepdims=True))
        prob = (expo / jnp.sum(expo, -1, keepdims=True)).astype(jnp.bfloat16)
        probs_ref[head] = prob
        attn_ref[:, lo:hi] = jnp.where(keep, mm(prob, v, NN), attn_ref[:, lo:hi])
    finish(started)
    resid = tok_ref[...].astype(jnp.float32) + mm(attn_ref[...].astype(jnp.bfloat16), w_ref[...], NT)
    resid_ref[...] = resid
    normed_ref[...] = norm_parts(resid)[0].astype(jnp.bfloat16)


def main_kernel(
    chips,
    height,
    width,
    normed_ref,
    resid_ref,
    target_ref,
    q_ref,
    kv_ref,
    probs_ref,
    *refs,
):
    mine, other, refs = split(refs, chips)
    owned, refs = refs[:2], refs[2:]
    rings = []
    for size in 2 * [mine_count(chips) - 1] + 2 * [other_count(chips) - 1]:
        rings.append(refs[:size])
        refs = refs[size:]
    (dq_ref, own_ref, low_ref, high_ref, dresid_ref, b_ref, o_ref, slope_ref, acc_ref, dkv_ref, sems) = refs
    inner = HS * HD
    group = lax.axis_index("groups")
    copies = []
    for i in range(4):
        row = pl.multiple_of(source_row("o", 0, chips, i >= 2) * height, 16)
        part = owned[i // 2].at[pl.ds(i % 2 * height, height), :]
        copies.append((part, b_ref.at[i % 2, pl.ds(row, height), :]))
    for i, block in enumerate(rings):
        dst = b_ref.at[group if i % 2 == 0 else 1 - group]
        copies += column_copies(block, dst, chips, height, width, 0, width, i >= 2, False)
    started = launch(copies, sems, 0)
    extra = column_copies(mine, o_ref, chips, height, width, 3 * inner, width, False, True)
    extra += column_copies(other, o_ref, chips, height, width, 3 * inner, width, True, True)
    later = launch(extra, sems, len(copies))
    finish(started)

    count = normed_ref.shape[0]
    hidden = width
    step = 2 * 256
    normed = normed_ref[...]
    acc_ref[...] = resid_ref[...] - target_ref[...]

    def forward(j, carry):
        cols = pl.ds(pl.multiple_of(j * step, step), step)
        pre = mm(normed, b_ref[0, :, cols], NN)
        cdf = 0.5 * (1.0 + lax.erf(pre * (1.0 / math.sqrt(2.0))))
        act = (pre * cdf).astype(jnp.bfloat16)
        slope_ref[:, cols] = cdf + pre * jnp.exp(-0.5 * pre * pre) * (1.0 / math.sqrt(2.0 * math.pi))
        acc_ref[...] += mm(act, b_ref[1, :, cols], NT)
        return carry

    lax.fori_loop(0, hidden // step, forward, 0)
    diff = acc_ref[...]
    dresid_ref[...] = diff
    diff_b = diff.astype(jnp.bfloat16)
    acc_ref[...] = jnp.zeros_like(acc_ref)

    def backward(j, carry):
        cols = pl.ds(pl.multiple_of(j * step, step), step)
        dact = mm(diff_b, b_ref[1, :, cols], NN)
        dpre = (dact * slope_ref[:, cols]).astype(jnp.bfloat16)
        acc_ref[...] += mm(dpre, b_ref[0, :, cols], NT)
        return carry

    lax.fori_loop(0, hidden // step, backward, 0)
    dresid = dresid_ref[...] + norm_back(resid_ref[...], acc_ref[...])
    dresid_ref[...] = dresid
    finish(later)
    dattn = mm(dresid.astype(jnp.bfloat16), o_ref[...], NN).astype(jnp.bfloat16)
    dkv_ref[...] = jnp.zeros_like(dkv_ref)
    dq_ref[...] = jnp.zeros_like(dq_ref)
    scale = 1.0 / math.sqrt(HD)
    zero = jnp.zeros((), jnp.bfloat16)
    for head in range(HS):
        lo, hi = head_window(head)
        keep = head_mask(head, count)
        q = jnp.where(keep, q_ref[:, lo:hi], zero)
        da = jnp.where(keep, dattn[:, lo:hi], zero)
        k = kv_ref[:, lo:hi]
        v = kv_ref[:, inner + lo : inner + hi]
        prob = probs_ref[head]
        prob_f = prob.astype(jnp.float32)
        dprob = mm(da, v, NT)
        delta = jnp.sum(prob_f * dprob, -1, keepdims=True)
        dscore = (prob_f * (dprob - delta)).astype(jnp.bfloat16)
        dq = (mm(dscore, k, NN) * scale).astype(jnp.bfloat16)
        dq_ref[:, lo:hi] = jnp.where(keep, dq, dq_ref[:, lo:hi])
        dkv_ref[:, lo:hi] += mm(dscore, q, TN) * scale
        dkv_ref[:, inner + lo : inner + hi] += mm(prob, da, TN)
    low_ref[...] = dkv_ref[0:count, :].astype(jnp.bfloat16)
    own_ref[...] = dkv_ref[count : 2 * count, :]
    high_ref[...] = dkv_ref[2 * count :, :].astype(jnp.bfloat16)


def final_kernel(
    chips, height, width, tok_ref, dresid_ref, dq_ref, own_ref, above_ref, below_ref, *refs
):
    mine, other, refs = split(refs, chips)
    out_ref, w_ref, sems = refs
    wide = w_ref.shape[1]
    copies = column_copies(mine, w_ref, chips, height, width, 0, wide, False, True)
    copies += column_copies(other, w_ref, chips, height, width, 0, wide, True, True)
    started = launch(copies, sems, 0)
    dkv = own_ref[...] + above_ref[...].astype(jnp.float32) + below_ref[...].astype(jnp.float32)
    dkv = dkv.astype(jnp.bfloat16)
    finish(started)
    inner = HS * HD
    dnorm = mm(dq_ref[...], w_ref[:, :inner], NT) + mm(dkv, w_ref[:, inner:], NT)
    out_ref[...] = dresid_ref[...] + norm_back(tok_ref[...].astype(jnp.float32), dnorm)


def body(mesh, tokens, teacher_qkv, s_qkv, s_out, mlp_in, mlp_out, t_out):
    return fast_body(mesh, tokens, teacher_qkv, s_qkv, s_out, mlp_in, mlp_out, t_out)


def fast_body(mesh, tokens, teacher_qkv, s_qkv, s_out, mlp_in, mlp_out, t_out):
    tile, cols, dim = tokens.shape
    devices = mesh.shape["rows"]
    chips = devices // 2
    count = tile * cols
    inner = HS * HD
    height = s_qkv.shape[0]
    width = mlp_in.shape[1]
    hidden = width
    bf, f32 = jnp.bfloat16, jnp.float32
    group = lax.axis_index("groups")
    partner = [(i, i ^ 1) for i in range(devices)]
    across = [(0, 1), (1, 0)]

    tok = tokens.reshape(count, dim)
    teacher = teacher_qkv.reshape(count, 3 * TH * HD)
    down = mlp_out.T
    b0 = jnp.where(group == 0, mlp_in, down)
    a0 = jnp.concatenate([s_qkv, s_out.T], axis=1)
    lanes = -(-3 * TH * HD // LANES) * LANES
    t_rows = jnp.pad(t_out.T, ((0, count - height), (0, lanes - 3 * TH * HD)))
    t0 = jnp.concatenate([teacher[:, TH * HD :], t_rows], axis=1)
    tq = jnp.pad(teacher[:, : TH * HD], ((0, 0), (0, lanes - TH * HD)))

    bu, bd = ring(b0, chips, 1)
    au, ad = ring(a0, chips, 1)
    tu, td = ring(t0, chips, 0)
    xu = [lax.ppermute(x, "groups", across) for x in bu]
    xd = [lax.ppermute(x, "groups", across) for x in bd]

    def swap(ups, downs, dim):
        out = []
        for k, (up, down) in enumerate(zip(ups, downs)):
            both = jnp.concatenate([up, down], axis=0 if k + 1 < len(ups) else dim)
            out.append(lax.ppermute(both, "rows", partner))
        return out

    t_mine = [t0] + tu + td
    a_mine = [a0] + au + ad
    t_other = [lax.ppermute(t0, "rows", partner)] + swap(tu, td, 0)
    a_other = [lax.ppermute(a0, "rows", partner)] + swap(au, ad, 1)
    stacked = jnp.concatenate([mlp_in, down], axis=0)
    owned = [stacked, lax.ppermute(stacked, "rows", partner)]
    b_other = swap(bu, bd, 1)
    x_other = swap(xu, xd, 1)
    slots = mine_count(chips) + 1
    upward = [(i, i + 1) for i in range(devices - 1)]
    downward = [(i + 1, i) for i in range(devices - 1)]
    low = lax.ppermute(tok, "rows", upward)
    high = lax.ppermute(tok, "rows", downward)

    target = call(
        functools.partial(teacher_kernel, chips, count, height),
        jax.ShapeDtypeStruct((count, dim), f32),
        [
            pltpu.VMEM((devices * count, lanes), bf),
            pltpu.VMEM((dim, lanes), bf),
            pltpu.SemaphoreType.DMA((4 * slots,)),
        ],
        24,
        4 * TH * count * devices * count * lanes,
        2 * devices * count * lanes,
        t_mine + t_other,
        [tq],
    )
    query, key_val = call(
        functools.partial(qkv_kernel, chips, height, width),
        (
            jax.ShapeDtypeStruct((count, inner), bf),
            jax.ShapeDtypeStruct((3 * count, 2 * inner), bf),
        ),
        [pltpu.VMEM((dim, 3 * inner), bf), pltpu.SemaphoreType.DMA((2 * slots,))],
        16,
        2 * count * dim * 7 * inner,
        2 * dim * 3 * inner,
        a_mine + a_other,
        [tok, low, high],
    )
    probs, resid, normed2 = call(
        functools.partial(
            attention_kernel, chips, height, width, cols, tile, devices * tile
        ),
        (
            jax.ShapeDtypeStruct((HS, count, 3 * count), bf),
            jax.ShapeDtypeStruct((count, dim), f32),
            jax.ShapeDtypeStruct((count, dim), bf),
        ),
        [
            pltpu.VMEM((dim, inner), bf),
            pltpu.VMEM((count, inner), f32),
            pltpu.SemaphoreType.DMA((2 * slots,)),
        ],
        16,
        2 * count * dim * inner + 4 * HS * count * 3 * count * 2 * LANES,
        2 * dim * inner + 2 * HS * count * 3 * count,
        a_mine + a_other,
        [tok, query, key_val],
    )
    blocks = bu + bd + xu + xd + b_other + x_other
    dq, own, to_above, to_below, dresid = call(
        functools.partial(main_kernel, chips, height, width),
        (
            jax.ShapeDtypeStruct((count, inner), bf),
            jax.ShapeDtypeStruct((count, 2 * inner), f32),
            jax.ShapeDtypeStruct((count, 2 * inner), bf),
            jax.ShapeDtypeStruct((count, 2 * inner), bf),
            jax.ShapeDtypeStruct((count, dim), f32),
        ),
        [
            pltpu.VMEM((2, dim, hidden), bf),
            pltpu.VMEM((dim, inner), bf),
            pltpu.VMEM((count, hidden), f32),
            pltpu.VMEM((count, dim), f32),
            pltpu.VMEM((3 * count, 2 * inner), f32),
            pltpu.SemaphoreType.DMA((8 * slots,)),
        ],
        36,
        8 * count * dim * hidden,
        4 * dim * hidden,
        a_mine + a_other + owned + blocks,
        [normed2, resid, target, query, key_val, probs],
    )
    from_above = lax.ppermute(to_below, "rows", upward)
    from_below = lax.ppermute(to_above, "rows", downward)
    d_tokens = call(
        functools.partial(final_kernel, chips, height, width),
        jax.ShapeDtypeStruct((count, dim), f32),
        [pltpu.VMEM((dim, 3 * inner), bf), pltpu.SemaphoreType.DMA((2 * slots,))],
        20,
        2 * count * dim * 3 * inner,
        2 * dim * 3 * inner,
        a_mine + a_other,
        [tok, dresid, dq, own, from_above, from_below],
    )
    return d_tokens.reshape(tile, cols, dim)


def extended_2(block, sides, width):
    for axis, dim in sides:
        count = lax.axis_size(axis)
        forward = [(i, i + 1) for i in range(count - 1)]
        backward = [(target, source) for source, target in forward]
        low = lax.ppermute(
            lax.slice_in_dim(block, block.shape[dim] - width, None, axis=dim), axis, forward
        )
        high = lax.ppermute(lax.slice_in_dim(block, 0, width, axis=dim), axis, backward)
        block = jnp.concatenate([low, block, high], axis=dim)
    return block


def from_behind(value, axis, by):
    length = lax.axis_size(axis)
    pairs = [(i, i + by) for i in range(length) if 0 <= i + by < length]
    return lax.ppermute(value, axis, pairs)


def gelu_slope(values):
    return 0.5 * (1.0 + jax.scipy.special.erf(values / math.sqrt(2.0))) + values * jnp.exp(
        -0.5 * values * values
    ) / math.sqrt(2.0 * math.pi)


def plain_body(tokens, teacher_qkv, s_qkv, s_out, mlp_in, mlp_out, t_out):
    tile, cols = (tokens.shape[0], tokens.shape[1])
    width = HS * HD
    half = WIN // 2
    scale = 1.0 / math.sqrt(HD)
    count = tile * cols
    w_qkv, w_out, w_in, w_down, w_teach = (
        lax.all_gather(s_qkv, "rows", axis=0, tiled=True),
        lax.all_gather(s_out, "rows", axis=1, tiled=True),
        lax.all_gather(mlp_in, "rows", axis=0, tiled=True),
        lax.all_gather(mlp_out, "rows", axis=1, tiled=True),
        lax.all_gather(t_out, "rows", axis=1, tiled=True),
    )
    flat_x = tokens.astype(jnp.float32).reshape(count, D)
    normed = norm_parts(flat_x)[0].astype(jnp.bfloat16)
    packed = jnp.dot(normed, w_qkv, preferred_element_type=jnp.float32).astype(jnp.bfloat16)
    packed = packed.reshape(tile, cols, 3 * width)
    query = packed[:, :, :width].reshape(count, HS, HD)
    key_val = packed[:, :, width:]
    extended = extended_2(key_val, (("rows", 0),), half)
    extended = jnp.pad(extended, ((0, 0), (half, half), (0, 0)))
    key_rows = tile + 2 * half
    key_cols = cols + 2 * half
    key_count = key_rows * key_cols
    both = extended.reshape(key_count, 2, HS, HD)
    keys_all = both[:, 0]
    vals_all = both[:, 1]
    query_row = (jnp.arange(count) // cols)[:, None]
    query_col = (jnp.arange(count) % cols)[:, None]
    key_row = (jnp.arange(key_count) // key_cols)[None, :]
    key_col = (jnp.arange(key_count) % key_cols)[None, :]
    row_off = key_row - half - query_row
    col_off = key_col - half - query_col
    global_row = lax.axis_index("rows") * tile + query_row + row_off
    valid = (row_off >= -half) & (row_off < half) & (col_off >= -half) & (col_off < half)
    valid = valid & (global_row >= 0) & (global_row < lax.axis_size("rows") * tile)
    valid = valid & (query_col + col_off >= 0) & (query_col + col_off < cols)
    scores = jnp.einsum("qhd,khd->hqk", query, keys_all, preferred_element_type=jnp.float32) * scale
    scores = jnp.where(valid[None], scores, -jnp.inf)
    peak = jnp.max(scores, -1, keepdims=True)
    expo = jnp.exp(scores - peak)
    probs = (expo / jnp.sum(expo, -1, keepdims=True)).astype(jnp.bfloat16)
    attn = jnp.einsum("hqk,khd->qhd", probs, vals_all, preferred_element_type=jnp.float32)
    attn = attn.astype(jnp.bfloat16).reshape(count, width)
    resid = flat_x + jnp.dot(attn, w_out, preferred_element_type=jnp.float32)
    teacher = teacher_qkv.reshape(count, 3 * TH * HD)
    t_query = teacher[:, : TH * HD].reshape(count, TH, HD)
    t_pairs = teacher[:, TH * HD :]
    piece = lax.all_gather(t_pairs, "rows", axis=0, tiled=True)
    run_max = jnp.full((TH, count), -1e30, jnp.float32)
    piece_kv = piece.reshape(piece.shape[0], 2, TH, HD)
    tscore = (
        jnp.einsum("qhd,khd->hqk", t_query, piece_kv[:, 0], preferred_element_type=jnp.float32)
        * scale
    )
    new_max = jnp.maximum(run_max, jnp.max(tscore, -1))
    expo_t = jnp.exp(tscore - new_max[..., None])
    new_total = jnp.sum(expo_t, -1)
    added = jnp.einsum(
        "hqk,khd->qhd",
        expo_t.astype(jnp.bfloat16),
        piece_kv[:, 1],
        preferred_element_type=jnp.float32,
    )
    t_att = (
        (added / jnp.transpose(new_total)[:, :, None]).astype(jnp.bfloat16).reshape(count, TH * HD)
    )
    target = jnp.dot(t_att, w_teach, preferred_element_type=jnp.float32)
    normed2 = norm_parts(resid)[0].astype(jnp.bfloat16)
    pre = jnp.dot(normed2, w_in, preferred_element_type=jnp.float32)
    act = jax.nn.gelu(pre, approximate=False).astype(jnp.bfloat16)
    student = resid + jnp.dot(act, w_down, preferred_element_type=jnp.float32)
    diff = student - target
    diff_b = diff.astype(jnp.bfloat16)
    dact = jnp.einsum("nd,hd->nh", diff_b, w_down, preferred_element_type=jnp.float32)
    dpre = (dact * gelu_slope(pre)).astype(jnp.bfloat16)
    dnorm2 = jnp.einsum("nh,dh->nd", dpre, w_in, preferred_element_type=jnp.float32)
    dresid = diff + norm_back(resid, dnorm2)
    dattn = jnp.einsum(
        "nd,ad->na", dresid.astype(jnp.bfloat16), w_out, preferred_element_type=jnp.float32
    )
    dattn = dattn.astype(jnp.bfloat16).reshape(count, HS, HD)
    dprob = jnp.einsum("qhd,khd->hqk", dattn, vals_all, preferred_element_type=jnp.float32)
    delta = jnp.sum(probs.astype(jnp.float32) * dprob, -1, keepdims=True)
    dscore = (probs.astype(jnp.float32) * (dprob - delta)).astype(jnp.bfloat16)
    dquery = (
        jnp.einsum("hqk,khd->qhd", dscore, keys_all, preferred_element_type=jnp.float32) * scale
    )
    dkey = jnp.einsum("hqk,qhd->khd", dscore, query, preferred_element_type=jnp.float32) * scale
    dval = jnp.einsum("hqk,qhd->khd", probs, dattn, preferred_element_type=jnp.float32)
    grad_kv = jnp.concatenate(
        [dkey.reshape(key_count, width), dval.reshape(key_count, width)], axis=-1
    )
    grad_kv = grad_kv.reshape(key_rows, key_cols, 2 * width)[:, half : half + cols]
    top_rim = grad_kv[:half].astype(jnp.bfloat16)
    bottom_rim = grad_kv[half + tile :].astype(jnp.bfloat16)
    own_rows = grad_kv[half : half + tile]
    from_above = from_behind(bottom_rim, "rows", 1)
    from_below = from_behind(top_rim, "rows", -1)
    own_rows = own_rows.at[:half].add(from_above.astype(jnp.float32))
    own_rows = own_rows.at[tile - half :].add(from_below.astype(jnp.float32))
    dqkv = jnp.concatenate(
        [dquery.reshape(count, width), own_rows.reshape(count, 2 * width)], axis=-1
    ).astype(jnp.bfloat16)
    dnorm = jnp.einsum("ne,de->nd", dqkv, w_qkv, preferred_element_type=jnp.float32)
    d_tokens = dresid + norm_back(flat_x, dnorm)
    return d_tokens.reshape(tile, cols, D)


def fits(mesh, shapes):
    devices = mesh.shape["rows"]
    return (
        mesh.shape["groups"] == 2
        and devices % 4 == 0
        and D % (16 * devices) == 0
        and shapes == WIN // 2
    )


def solution(mesh):
    placed = (
        P(("groups", "rows"), None, None),
        P(("groups", "rows"), None, None),
        P("rows", None),
        P(None, "rows"),
        P("rows", None),
        P(None, "rows"),
        P(None, "rows"),
    )

    def chosen(tokens, *rest):
        tile = tokens.shape[0] // (mesh.shape["groups"] * mesh.shape["rows"])
        fast = fits(mesh, tile)
        step = jax.shard_map(
            functools.partial(body, mesh) if fast else plain_body,
            mesh=mesh,
            in_specs=placed,
            out_specs=P(("groups", "rows"), None, None),
            check_vma=False,
        )
        return step(tokens, *rest)

    return chosen
```

```python
import functools
import math

import jax
import jax.numpy as jnp
from jax import lax
from jax.experimental import pallas as pl
from jax.experimental.pallas import tpu as pltpu
from jax.sharding import PartitionSpec as P


D = 1280
HS = 8
HD = 80
TH = 2
WIN = 8
LANES = 128


EPS = 1e-06


NN = (((1,), (0,)), ((), ()))
NT = (((1,), (1,)), ((), ()))
TN = (((0,), (0,)), ((), ()))


def mm(left, right, dims):
    return lax.dot_general(left, right, dims, preferred_element_type=jnp.float32)


def norm_parts(values):
    centre = values - jnp.mean(values, -1, keepdims=True)
    inverse = lax.rsqrt(jnp.mean(centre * centre, -1, keepdims=True) + EPS)
    return centre * inverse, inverse


def norm_back(values, grads):
    normed, inverse = norm_parts(values)
    return inverse * (
        grads
        - jnp.mean(grads, -1, keepdims=True)
        - normed * jnp.mean(grads * normed, -1, keepdims=True)
    )


def chip_at(place, chips):
    return 2 * place if place < chips // 2 else 2 * (chips - 1 - place) + 1


def ring_pairs(chips, step):
    pairs = []
    for place in range(chips):
        source, target = chip_at(place, chips), chip_at((place + step) % chips, chips)
        pairs += [(2 * source + core, 2 * target + core) for core in range(2)]
    return pairs


def ring(piece, chips, dim):
    forward, backward = ring_pairs(chips, 1), ring_pairs(chips, -1)
    reach = chips // 2
    cut = piece.shape[dim] // 2
    ups, downs = [piece], [piece]
    for _ in range(1, reach):
        ups.append(lax.ppermute(ups[-1], "rows", forward))
        downs.append(lax.ppermute(downs[-1], "rows", backward))
    last_up = lax.slice_in_dim(ups[-1], 0, cut, axis=dim)
    last_down = lax.slice_in_dim(downs[-1], cut, None, axis=dim)
    ups.append(lax.ppermute(last_up, "rows", forward))
    downs.append(lax.ppermute(last_down, "rows", backward))
    return ups[1:], downs[1:]


def mine_count(chips):
    return 1 + chips // 2 * 2


def other_count(chips):
    return 1 + chips // 2


def source_row(kind, k, chips, swap):
    me = lax.axis_index("rows")
    chip, core = lax.div(me, 2), lax.rem(me, 2)
    level = lax.div(chip, 2)
    place = jnp.where(lax.rem(chip, 2) == 0, level, chips - 1 - level)
    shift = {"o": 0, "u": chips - k, "d": k, "f": k}[kind]
    at = lax.rem(place + shift, chips)
    source = jnp.where(at < chips // 2, 2 * at, 2 * (chips - 1 - at) + 1)
    return 2 * source + (1 - core if swap else core)


def pieces(refs, chips, merged, own):
    reach = chips // 2
    out = []
    refs = list(refs)
    if own:
        out.append(("o", 0, refs.pop(0)))
    if not merged:
        slots = [("u", k) for k in range(1, reach + 1)] + [("d", k) for k in range(1, reach + 1)]
        return out + [(kind, k, ref) for (kind, k), ref in zip(slots, refs)]
    for k, ref in zip(range(1, reach), refs):
        rows = ref.shape[0] // 2
        out += [("u", k, ref.at[0:rows]), ("d", k, ref.at[rows : 2 * rows])]
    return out + [("f", reach, refs[-1])]


def piece_copies(refs, dst, chips, height, merged, own):
    out = []
    for kind, k, ref in pieces(refs, chips, merged, own):
        row = source_row(kind, k, chips, merged) * height
        width = ref.shape[1]
        first = dst.shape[1] - width if kind == "d" and k == chips // 2 else 0
        out.append((ref, dst.at[:, first : first + width], row))
    return out


def row_copies(refs, dst, chips, total, keep, lo, merged):
    out = []
    for kind, k, ref in pieces(refs, chips, merged, True):
        first, last = 0, total
        if k == chips // 2 and kind != "f":
            first, last = (0, total // 2) if kind == "u" else (total // 2, total)
        stop = min(keep, last)
        if first < stop:
            row = source_row(kind, k, chips, merged) * keep + first
            out.append((ref.at[0 : stop - first, lo:], dst, row))
    return out


def carry_out(copies):
    for src, dst, row in copies:
        rows = src.shape[0]
        step = math.gcd(rows, 16)

        def move(i, carry, src=src, dst=dst, row=row, step=step):
            here = pl.multiple_of(i * step, step)
            there = pl.multiple_of(row + i * step, step)
            dst[pl.ds(there, step), :] = src[pl.ds(here, step), :]
            return carry

        lax.fori_loop(0, rows // step, move, 0)


VM = pl.BlockSpec(memory_space=pltpu.VMEM)


def call(kernel, outs, scratch, vmem_mib, flops, moved, args, aliases=None):
    return pl.pallas_call(
        kernel,
        out_shape=outs,
        in_specs=[VM] * len(args),
        out_specs=jax.tree.map(lambda _: VM, outs),
        scratch_shapes=scratch,
        input_output_aliases=aliases or {},
        cost_estimate=pl.CostEstimate(flops=flops, transcendentals=0, bytes_accessed=moved),
        compiler_params=pltpu.CompilerParams(vmem_limit_bytes=vmem_mib << 20),
    )(*args)


def head_window(head):
    first, last = head * HD, (head + 1) * HD
    lo, hi = first // LANES * LANES, -(-last // LANES) * LANES
    return lo, hi


def head_mask(head, rows):
    lo, hi = head_window(head)
    lane = lax.broadcasted_iota(jnp.int32, (rows, hi - lo), 1) + lo
    return (lane >= head * HD) & (lane < (head + 1) * HD)


def split(refs, chips):
    n, m = mine_count(chips), other_count(chips)
    return refs[:n], refs[n : n + m], refs[n + m :]


def qkv_kernel(chips, height, tok_ref, lo_ref, hi_ref, *refs):
    mine, other, refs = split(refs, chips)
    q_ref, kv_ref, w_ref = refs
    carry_out(piece_copies(mine, w_ref, chips, height, False, True))
    carry_out(piece_copies(other, w_ref, chips, height, True, True))
    normed = [
        norm_parts(ref[...].astype(jnp.float32))[0].astype(jnp.bfloat16)
        for ref in (lo_ref, tok_ref, hi_ref)
    ]
    inner = HS * HD
    q_ref[...] = mm(normed[1], w_ref[:, :inner], NN).astype(jnp.bfloat16)
    rows = jnp.concatenate(normed, axis=0)
    for part in range(2):
        cols = slice(part * inner, (part + 1) * inner)
        weights = w_ref[:, (part + 1) * inner : (part + 2) * inner]
        kv_ref[:, cols] = mm(rows, weights, NN).astype(jnp.bfloat16)


def teacher_kernel(chips, rows, height, tq_ref, *refs):
    mine, other, refs = split(refs, chips)
    target_ref, out_ref, score_ref = refs
    width = TH * HD
    near = -(-width // LANES) * LANES
    lo, hi = width // LANES * LANES, -(-2 * width // LANES) * LANES
    far = 2 * width // LANES * LANES
    carry_out(row_copies(mine, out_ref, chips, rows, height, far, False))
    carry_out(row_copies(other, out_ref, chips, rows, height, far, True))
    query = tq_ref[:, :near]
    lane = lax.broadcasted_iota(jnp.int32, query.shape, 1)
    heads = [(lane >= head * HD) & (lane < (head + 1) * HD) for head in range(TH)]
    own = jnp.concatenate([jnp.where(here, query, jnp.zeros_like(query)) for here in heads], axis=0)
    blocks, size = [[]], 0
    for ref in list(mine) + list(other):
        if size >= 4 * rows:
            blocks.append([])
            size = 0
        blocks[-1].append(ref)
        size += ref.shape[0]
    spans, base = [], 0
    for block in blocks:
        size = sum(ref.shape[0] for ref in block)
        spans.append(slice(base, base + size))
        base += size

    def keys_of(block, first, last):
        return jnp.concatenate([ref[:, first:last] for ref in block], axis=0)

    peak = None
    for block, keys in zip(blocks, spans):
        score = mm(own, keys_of(block, 0, near), NT) * (1.0 / math.sqrt(HD))
        score_ref[:, keys] = score
        top = jnp.max(score, -1, keepdims=True)
        peak = top if peak is None else jnp.maximum(peak, top)
    summed, value = 0.0, 0.0
    for block, keys in zip(blocks, spans):
        expo = jnp.exp(score_ref[:, keys] - peak)
        summed = summed + jnp.sum(expo, -1, keepdims=True)
        value = value + mm(expo.astype(jnp.bfloat16), keys_of(block, lo, hi), NN)
    value = value / summed
    lane = lax.broadcasted_iota(jnp.int32, (rows, hi - lo), 1) + lo - width
    att = jnp.zeros((rows, hi - lo), jnp.float32)
    for head in range(TH):
        here = (lane >= head * HD) & (lane < (head + 1) * HD)
        att = jnp.where(here, value[head * rows : (head + 1) * rows], att)
    shift = (2 * width - far) - (width - lo)
    spread = pltpu.roll(att, shift % (hi - lo), axis=1).astype(jnp.bfloat16)
    target_ref[...] = mm(spread, out_ref[...], NT)


def near_mask(count, cols, tile, last):
    half = WIN // 2
    shape = (count, 3 * count)
    query = lax.broadcasted_iota(jnp.int32, shape, 0)
    key = lax.broadcasted_iota(jnp.int32, shape, 1)
    row_off = lax.div(key, cols) - tile - lax.div(query, cols)
    col_off = lax.rem(key, cols) - lax.rem(query, cols)
    me = lax.axis_index("rows")
    row = me * tile + lax.div(key, cols) - tile
    valid = (row_off >= -half) & (row_off < half) & (col_off >= -half) & (col_off < half)
    return valid & (row >= 0) & (row < last)


def attention_kernel(
    cols, tile, last, tok_ref, q_ref, kv_ref, w_ref, probs_ref, resid_ref, normed_ref, attn_ref
):
    inner = HS * HD
    count = q_ref.shape[0]
    valid = near_mask(count, cols, tile, last)
    attn_ref[...] = jnp.zeros_like(attn_ref)
    for head in range(HS):
        lo, hi = head_window(head)
        keep = head_mask(head, count)
        q = jnp.where(keep, q_ref[:, lo:hi], jnp.zeros((), jnp.bfloat16))
        k = kv_ref[:, lo:hi]
        v = kv_ref[:, inner + lo : inner + hi]
        score = jnp.where(valid, mm(q, k, NT) * (1.0 / math.sqrt(HD)), -jnp.inf)
        expo = jnp.exp(score - jnp.max(score, -1, keepdims=True))
        prob = (expo / jnp.sum(expo, -1, keepdims=True)).astype(jnp.bfloat16)
        probs_ref[head] = prob
        attn_ref[:, lo:hi] = jnp.where(keep, mm(prob, v, NN), attn_ref[:, lo:hi])
    attn = attn_ref[...].astype(jnp.bfloat16)
    resid = tok_ref[...].astype(jnp.float32) + mm(attn, w_ref[:, 3 * inner :], NT)
    resid_ref[...] = resid
    normed_ref[...] = norm_parts(resid)[0].astype(jnp.bfloat16)


def pack_kernel(chips, height, *refs):
    reach = chips // 2
    owned, refs = refs[:2], refs[2:]
    ring_mine, refs = refs[: 2 * reach], refs[2 * reach :]
    across, refs = refs[: 2 * reach - 2], refs[2 * reach - 2 :]
    ring_other, refs = refs[:reach], refs[reach:]
    across_other, (b_ref,) = refs[: reach - 1], refs[reach - 1 :]
    group = lax.axis_index("groups")
    copies = []
    for i in range(4):
        row = source_row("o", 0, chips, i >= 2) * height
        copies.append((owned[i // 2].at[i % 2 * height : (i % 2 + 1) * height], b_ref.at[i % 2], row))
    copies += piece_copies(ring_mine, b_ref.at[group], chips, height, False, False)
    copies += piece_copies(ring_other, b_ref.at[group], chips, height, True, False)
    for k in range(1, reach):
        views = [
            ("u", False, across[k - 1]),
            ("d", False, across[reach + k - 2]),
            ("u", True, across_other[k - 1].at[0:height]),
            ("d", True, across_other[k - 1].at[height : 2 * height]),
        ]
        for kind, merged, ref in views:
            copies.append((ref, b_ref.at[1 - group], source_row(kind, k, chips, merged) * height))
    carry_out(copies)


def main_kernel(
    chips,
    height,
    normed_ref,
    resid_ref,
    target_ref,
    q_ref,
    kv_ref,
    probs_ref,
    w_ref,
    last_up_ref,
    last_down_ref,
    last_other_ref,
    given_ref,
    dq_ref,
    own_ref,
    low_ref,
    high_ref,
    dresid_ref,
    b_ref,
    act_ref,
    slope_ref,
    acc_ref,
    dkv_ref,
):
    reach = chips // 2
    inner = HS * HD
    hidden = b_ref.shape[2]
    parts = 5
    step = hidden // parts
    dst = b_ref.at[1 - lax.axis_index("groups")]
    half = hidden // 2
    row = source_row("f", reach, chips, False) * height
    copies = [
        (last_up_ref, dst.at[:, :half], row),
        (last_down_ref, dst.at[:, half:], row),
        (last_other_ref, dst, source_row("f", reach, chips, True) * height),
    ]
    carry_out(copies)
    count = normed_ref.shape[0]
    normed = normed_ref[...]
    for j in range(parts):
        cols = slice(j * step, (j + 1) * step)
        pre = mm(normed, b_ref[0, :, cols], NN)
        cdf = 0.5 * (1.0 + lax.erf(pre * (1.0 / math.sqrt(2.0))))
        act_ref[:, cols] = (pre * cdf).astype(jnp.bfloat16)
        slope_ref[:, cols] = cdf + pre * jnp.exp(-0.5 * pre * pre) * (1.0 / math.sqrt(2.0 * math.pi))
    acc_ref[...] = resid_ref[...] - target_ref[...] + mm(act_ref[...], b_ref[1], NT)
    diff = acc_ref[...]
    dresid_ref[...] = diff
    diff_b = diff.astype(jnp.bfloat16)
    for j in range(parts):
        cols = slice(j * step, (j + 1) * step)
        dact = mm(diff_b, b_ref[1, :, cols], NN)
        act_ref[:, cols] = (dact * slope_ref[:, cols]).astype(jnp.bfloat16)
    acc_ref[...] = mm(act_ref[...], b_ref[0], NT)
    dresid = dresid_ref[...] + norm_back(resid_ref[...], acc_ref[...])
    dresid_ref[...] = dresid
    dattn = mm(dresid.astype(jnp.bfloat16), w_ref[:, 3 * inner :], NN).astype(jnp.bfloat16)
    dkv_ref[...] = jnp.zeros_like(dkv_ref)
    dq_ref[...] = jnp.zeros_like(dq_ref)
    scale = 1.0 / math.sqrt(HD)
    zero = jnp.zeros((), jnp.bfloat16)
    for head in range(HS):
        lo, hi = head_window(head)
        keep = head_mask(head, count)
        q = jnp.where(keep, q_ref[:, lo:hi], zero)
        da = jnp.where(keep, dattn[:, lo:hi], zero)
        k = kv_ref[:, lo:hi]
        v = kv_ref[:, inner + lo : inner + hi]
        prob = probs_ref[head]
        prob_f = prob.astype(jnp.float32)
        dprob = mm(da, v, NT)
        delta = jnp.sum(prob_f * dprob, -1, keepdims=True)
        dscore = (prob_f * (dprob - delta)).astype(jnp.bfloat16)
        dq = (mm(dscore, k, NN) * scale).astype(jnp.bfloat16)
        dq_ref[:, lo:hi] = jnp.where(keep, dq, dq_ref[:, lo:hi])
        dkv_ref[:, lo:hi] += mm(dscore, q, TN) * scale
        dkv_ref[:, inner + lo : inner + hi] += mm(prob, da, TN)
    low_ref[...] = dkv_ref[0:count, :].astype(jnp.bfloat16)
    own_ref[...] = dkv_ref[count : 2 * count, :]
    high_ref[...] = dkv_ref[2 * count :, :].astype(jnp.bfloat16)


def final_kernel(
    tok_ref, dresid_ref, dq_ref, own_ref, above_ref, below_ref, w_ref, out_ref
):
    dkv = own_ref[...] + above_ref[...].astype(jnp.float32) + below_ref[...].astype(jnp.float32)
    dkv = dkv.astype(jnp.bfloat16)
    inner = HS * HD
    dnorm = mm(dq_ref[...], w_ref[:, :inner], NT) + mm(dkv, w_ref[:, inner : 3 * inner], NT)
    out_ref[...] = dresid_ref[...] + norm_back(tok_ref[...].astype(jnp.float32), dnorm)


def body(mesh, tokens, teacher_qkv, s_qkv, s_out, mlp_in, mlp_out, t_out):
    return fast_body(mesh, tokens, teacher_qkv, s_qkv, s_out, mlp_in, mlp_out, t_out)


def fast_body(mesh, tokens, teacher_qkv, s_qkv, s_out, mlp_in, mlp_out, t_out):
    tile, cols, dim = tokens.shape
    devices = mesh.shape["rows"]
    chips = devices // 2
    count = tile * cols
    inner = HS * HD
    height = s_qkv.shape[0]
    width = mlp_in.shape[1]
    hidden = width
    bf, f32 = jnp.bfloat16, jnp.float32
    group = lax.axis_index("groups")
    partner = [(i, i ^ 1) for i in range(devices)]
    across = [(0, 1), (1, 0)]

    tok = tokens.reshape(count, dim)
    teacher = teacher_qkv.reshape(count, 3 * TH * HD)
    down = mlp_out.T
    b0 = jnp.where(group == 0, mlp_in, down)
    a0 = jnp.concatenate([s_qkv, s_out.T], axis=1)
    lanes = -(-3 * TH * HD // LANES) * LANES
    t_rows = jnp.pad(t_out.T, ((0, count - height), (0, lanes - 3 * TH * HD)))
    t0 = jnp.concatenate([teacher[:, TH * HD :], t_rows], axis=1)
    tq = jnp.pad(teacher[:, : TH * HD], ((0, 0), (0, lanes - TH * HD)))

    bu, bd = ring(b0, chips, 1)
    au, ad = ring(a0, chips, 1)
    tu, td = ring(t0, chips, 0)
    xu = [lax.ppermute(x, "groups", across) for x in bu]
    xd = [lax.ppermute(x, "groups", across) for x in bd]

    def swap(ups, downs, dim):
        out = []
        for k, (up, down) in enumerate(zip(ups, downs)):
            both = jnp.concatenate([up, down], axis=0 if k + 1 < len(ups) else dim)
            out.append(lax.ppermute(both, "rows", partner))
        return out

    t_mine = [t0] + tu + td
    a_mine = [a0] + au + ad
    t_other = [lax.ppermute(t0, "rows", partner)] + swap(tu, td, 0)
    a_other = [lax.ppermute(a0, "rows", partner)] + swap(au, ad, 1)
    stacked = jnp.concatenate([mlp_in, down], axis=0)
    owned = [stacked, lax.ppermute(stacked, "rows", partner)]
    b_other = swap(bu, bd, 1)
    x_other = swap(xu, xd, 1)
    upward = [(i, i + 1) for i in range(devices - 1)]
    downward = [(i + 1, i) for i in range(devices - 1)]
    low = lax.ppermute(tok, "rows", upward)
    high = lax.ppermute(tok, "rows", downward)

    target = call(
        functools.partial(teacher_kernel, chips, count, height),
        jax.ShapeDtypeStruct((count, dim), f32),
        [
            pltpu.VMEM((dim, lanes - 2 * TH * HD // LANES * LANES), bf),
            pltpu.VMEM((TH * count, devices * count), f32),
        ],
        10,
        4 * TH * count * devices * count * lanes,
        2 * devices * count * lanes,
        [tq] + t_mine + t_other,
    )
    query, key_val, weights = call(
        functools.partial(qkv_kernel, chips, height),
        (
            jax.ShapeDtypeStruct((count, inner), bf),
            jax.ShapeDtypeStruct((3 * count, 2 * inner), bf),
            jax.ShapeDtypeStruct((dim, width), bf),
        ),
        [],
        10,
        2 * count * dim * 7 * inner,
        2 * dim * 3 * inner,
        [tok, low, high] + a_mine + a_other,
    )
    probs, resid, normed2 = call(
        functools.partial(attention_kernel, cols, tile, devices * tile),
        (
            jax.ShapeDtypeStruct((HS, count, 3 * count), bf),
            jax.ShapeDtypeStruct((count, dim), f32),
            jax.ShapeDtypeStruct((count, dim), bf),
        ),
        [pltpu.VMEM((count, inner), f32)],
        8,
        2 * count * dim * inner + 4 * HS * count * 3 * count * 2 * LANES,
        2 * dim * inner + 2 * HS * count * 3 * count,
        [tok, query, key_val, weights],
    )
    packed = call(
        functools.partial(pack_kernel, chips, height),
        jax.ShapeDtypeStruct((2, dim, hidden), bf),
        [],
        4,
        0,
        4 * dim * hidden,
        owned + bu + bd + xu[:-1] + xd[:-1] + b_other + x_other[:-1],
    )
    dq, own, to_above, to_below, dresid, _ = call(
        functools.partial(main_kernel, chips, height),
        (
            jax.ShapeDtypeStruct((count, inner), bf),
            jax.ShapeDtypeStruct((count, 2 * inner), f32),
            jax.ShapeDtypeStruct((count, 2 * inner), bf),
            jax.ShapeDtypeStruct((count, 2 * inner), bf),
            jax.ShapeDtypeStruct((count, dim), f32),
            jax.ShapeDtypeStruct((2, dim, hidden), bf),
        ),
        [
            pltpu.VMEM((count, hidden), bf),
            pltpu.VMEM((count, hidden), f32),
            pltpu.VMEM((count, dim), f32),
            pltpu.VMEM((3 * count, 2 * inner), f32),
        ],
        16,
        8 * count * dim * hidden,
        4 * dim * hidden,
        [normed2, resid, target, query, key_val, probs, weights]
        + [xu[-1], xd[-1], x_other[-1], packed],
        {10: 5},
    )
    from_above = lax.ppermute(to_below, "rows", upward)
    from_below = lax.ppermute(to_above, "rows", downward)
    d_tokens = call(
        final_kernel,
        jax.ShapeDtypeStruct((count, dim), f32),
        [],
        8,
        2 * count * dim * 3 * inner,
        2 * dim * 3 * inner,
        [tok, dresid, dq, own, from_above, from_below, weights],
    )
    return d_tokens.reshape(tile, cols, dim)


def extended_2(block, sides, width):
    for axis, dim in sides:
        count = lax.axis_size(axis)
        forward = [(i, i + 1) for i in range(count - 1)]
        backward = [(target, source) for source, target in forward]
        low = lax.ppermute(
            lax.slice_in_dim(block, block.shape[dim] - width, None, axis=dim), axis, forward
        )
        high = lax.ppermute(lax.slice_in_dim(block, 0, width, axis=dim), axis, backward)
        block = jnp.concatenate([low, block, high], axis=dim)
    return block


def from_behind(value, axis, by):
    length = lax.axis_size(axis)
    pairs = [(i, i + by) for i in range(length) if 0 <= i + by < length]
    return lax.ppermute(value, axis, pairs)


def gelu_slope(values):
    return 0.5 * (1.0 + jax.scipy.special.erf(values / math.sqrt(2.0))) + values * jnp.exp(
        -0.5 * values * values
    ) / math.sqrt(2.0 * math.pi)


def plain_body(tokens, teacher_qkv, s_qkv, s_out, mlp_in, mlp_out, t_out):
    tile, cols = (tokens.shape[0], tokens.shape[1])
    width = HS * HD
    half = WIN // 2
    scale = 1.0 / math.sqrt(HD)
    count = tile * cols
    w_qkv, w_out, w_in, w_down, w_teach = (
        lax.all_gather(s_qkv, "rows", axis=0, tiled=True),
        lax.all_gather(s_out, "rows", axis=1, tiled=True),
        lax.all_gather(mlp_in, "rows", axis=0, tiled=True),
        lax.all_gather(mlp_out, "rows", axis=1, tiled=True),
        lax.all_gather(t_out, "rows", axis=1, tiled=True),
    )
    flat_x = tokens.astype(jnp.float32).reshape(count, D)
    normed = norm_parts(flat_x)[0].astype(jnp.bfloat16)
    packed = jnp.dot(normed, w_qkv, preferred_element_type=jnp.float32).astype(jnp.bfloat16)
    packed = packed.reshape(tile, cols, 3 * width)
    query = packed[:, :, :width].reshape(count, HS, HD)
    key_val = packed[:, :, width:]
    extended = extended_2(key_val, (("rows", 0),), half)
    extended = jnp.pad(extended, ((0, 0), (half, half), (0, 0)))
    key_rows = tile + 2 * half
    key_cols = cols + 2 * half
    key_count = key_rows * key_cols
    both = extended.reshape(key_count, 2, HS, HD)
    keys_all = both[:, 0]
    vals_all = both[:, 1]
    query_row = (jnp.arange(count) // cols)[:, None]
    query_col = (jnp.arange(count) % cols)[:, None]
    key_row = (jnp.arange(key_count) // key_cols)[None, :]
    key_col = (jnp.arange(key_count) % key_cols)[None, :]
    row_off = key_row - half - query_row
    col_off = key_col - half - query_col
    global_row = lax.axis_index("rows") * tile + query_row + row_off
    valid = (row_off >= -half) & (row_off < half) & (col_off >= -half) & (col_off < half)
    valid = valid & (global_row >= 0) & (global_row < lax.axis_size("rows") * tile)
    valid = valid & (query_col + col_off >= 0) & (query_col + col_off < cols)
    scores = jnp.einsum("qhd,khd->hqk", query, keys_all, preferred_element_type=jnp.float32) * scale
    scores = jnp.where(valid[None], scores, -jnp.inf)
    peak = jnp.max(scores, -1, keepdims=True)
    expo = jnp.exp(scores - peak)
    probs = (expo / jnp.sum(expo, -1, keepdims=True)).astype(jnp.bfloat16)
    attn = jnp.einsum("hqk,khd->qhd", probs, vals_all, preferred_element_type=jnp.float32)
    attn = attn.astype(jnp.bfloat16).reshape(count, width)
    resid = flat_x + jnp.dot(attn, w_out, preferred_element_type=jnp.float32)
    teacher = teacher_qkv.reshape(count, 3 * TH * HD)
    t_query = teacher[:, : TH * HD].reshape(count, TH, HD)
    t_pairs = teacher[:, TH * HD :]
    piece = lax.all_gather(t_pairs, "rows", axis=0, tiled=True)
    run_max = jnp.full((TH, count), -1e30, jnp.float32)
    piece_kv = piece.reshape(piece.shape[0], 2, TH, HD)
    tscore = (
        jnp.einsum("qhd,khd->hqk", t_query, piece_kv[:, 0], preferred_element_type=jnp.float32)
        * scale
    )
    new_max = jnp.maximum(run_max, jnp.max(tscore, -1))
    expo_t = jnp.exp(tscore - new_max[..., None])
    new_total = jnp.sum(expo_t, -1)
    added = jnp.einsum(
        "hqk,khd->qhd",
        expo_t.astype(jnp.bfloat16),
        piece_kv[:, 1],
        preferred_element_type=jnp.float32,
    )
    t_att = (
        (added / jnp.transpose(new_total)[:, :, None]).astype(jnp.bfloat16).reshape(count, TH * HD)
    )
    target = jnp.dot(t_att, w_teach, preferred_element_type=jnp.float32)
    normed2 = norm_parts(resid)[0].astype(jnp.bfloat16)
    pre = jnp.dot(normed2, w_in, preferred_element_type=jnp.float32)
    act = jax.nn.gelu(pre, approximate=False).astype(jnp.bfloat16)
    student = resid + jnp.dot(act, w_down, preferred_element_type=jnp.float32)
    diff = student - target
    diff_b = diff.astype(jnp.bfloat16)
    dact = jnp.einsum("nd,hd->nh", diff_b, w_down, preferred_element_type=jnp.float32)
    dpre = (dact * gelu_slope(pre)).astype(jnp.bfloat16)
    dnorm2 = jnp.einsum("nh,dh->nd", dpre, w_in, preferred_element_type=jnp.float32)
    dresid = diff + norm_back(resid, dnorm2)
    dattn = jnp.einsum(
        "nd,ad->na", dresid.astype(jnp.bfloat16), w_out, preferred_element_type=jnp.float32
    )
    dattn = dattn.astype(jnp.bfloat16).reshape(count, HS, HD)
    dprob = jnp.einsum("qhd,khd->hqk", dattn, vals_all, preferred_element_type=jnp.float32)
    delta = jnp.sum(probs.astype(jnp.float32) * dprob, -1, keepdims=True)
    dscore = (probs.astype(jnp.float32) * (dprob - delta)).astype(jnp.bfloat16)
    dquery = (
        jnp.einsum("hqk,khd->qhd", dscore, keys_all, preferred_element_type=jnp.float32) * scale
    )
    dkey = jnp.einsum("hqk,qhd->khd", dscore, query, preferred_element_type=jnp.float32) * scale
    dval = jnp.einsum("hqk,qhd->khd", probs, dattn, preferred_element_type=jnp.float32)
    grad_kv = jnp.concatenate(
        [dkey.reshape(key_count, width), dval.reshape(key_count, width)], axis=-1
    )
    grad_kv = grad_kv.reshape(key_rows, key_cols, 2 * width)[:, half : half + cols]
    top_rim = grad_kv[:half].astype(jnp.bfloat16)
    bottom_rim = grad_kv[half + tile :].astype(jnp.bfloat16)
    own_rows = grad_kv[half : half + tile]
    from_above = from_behind(bottom_rim, "rows", 1)
    from_below = from_behind(top_rim, "rows", -1)
    own_rows = own_rows.at[:half].add(from_above.astype(jnp.float32))
    own_rows = own_rows.at[tile - half :].add(from_below.astype(jnp.float32))
    dqkv = jnp.concatenate(
        [dquery.reshape(count, width), own_rows.reshape(count, 2 * width)], axis=-1
    ).astype(jnp.bfloat16)
    dnorm = jnp.einsum("ne,de->nd", dqkv, w_qkv, preferred_element_type=jnp.float32)
    d_tokens = dresid + norm_back(flat_x, dnorm)
    return d_tokens.reshape(tile, cols, D)


def fits(mesh, shapes):
    devices = mesh.shape["rows"]
    return (
        mesh.shape["groups"] == 2
        and devices % 4 == 0
        and D % (16 * devices) == 0
        and shapes == WIN // 2
    )


def solution(mesh):
    placed = (
        P(("groups", "rows"), None, None),
        P(("groups", "rows"), None, None),
        P("rows", None),
        P(None, "rows"),
        P("rows", None),
        P(None, "rows"),
        P(None, "rows"),
    )

    def chosen(tokens, *rest):
        tile = tokens.shape[0] // (mesh.shape["groups"] * mesh.shape["rows"])
        fast = fits(mesh, tile)
        step = jax.shard_map(
            functools.partial(body, mesh) if fast else plain_body,
            mesh=mesh,
            in_specs=placed,
            out_specs=P(("groups", "rows"), None, None),
            check_vma=False,
        )
        return step(tokens, *rest)

    return chosen
```
